256 devices in a mesh: gr: 8 (over x, core), gc: 32 (over z, y).
Axes of the slice: x: 4, y: 4, z: 8, core: 2. Of those that a mesh axis runs over, the one named last changes fastest.
Arguments:
- factor_window: bfloat16 [26624, 8192], P('gr', 'gc'), may hold values from -0.0625 to 0.0625
- upper_panel: bfloat16 [8192, 512], P('gc', 'gr'), may hold values from -6 to 6
- panel_block: float32 [26624, 512], P(('gr', 'gc'))
- first_block: int32 [64], P('gc'), may hold values from 0 to 104
Outputs:
- panel_factor: float32 [26624, 512], P(('gr', 'gc'))
The draws below stay inside these ranges and needn't reach their ends.
All inputs are finite; a program needn't handle non-finite values.
Results may differ from the reference program's by a relative error of at most 0.0003.
Values may be sent and summed in bfloat16 or wider, within the bound.
A program may use at most 64 MiB of HBM per device.

```python
import math
import jax
import jax.numpy as jnp
from jax import lax

PW = 512
BLK = 128
KC_DEV = 256
MR_DEV = 3328
NS_ITERS = 3
ROWS = 26624
COLS = 8192
N_GR = 8
N_GC = 32


def draw_panel_block(key, part):
    array_shape = (MR_DEV * N_GR, PW)
    entries = jax.random.normal(key, array_shape, jnp.float32)
    row_ids = lax.broadcasted_iota(jnp.int32, array_shape, 0)
    col_ids = lax.broadcasted_iota(jnp.int32, array_shape, 1)
    shift = 6.0 * math.sqrt(PW)
    return entries + jnp.where(row_ids == col_ids, shift, 0.0).astype(jnp.float32)


def draw_first_block(key, part):
    blocks = KC_DEV * N_GC // BLK
    highest = MR_DEV * N_GR // (2 * BLK)
    values = jax.random.randint(jax.random.fold_in(key, 1), (blocks,), 0, highest + 1, dtype=jnp.int32)
    order = jax.random.permutation(jax.random.fold_in(key, 2), blocks)
    values = values.at[order[0]].set(highest)
    values = values.at[order[1]].set(0)
    return values.astype(jnp.int32)


def shard_levels(key, dims, split, low, top_value):
    level = 1.0
    for dim, shards_of in split:
        draws = jax.random.uniform(jax.random.fold_in(jax.random.fold_in(key, 6), dim), (shards_of,), jnp.float32, low / len(split), top_value / len(split))
        level = level * jnp.repeat(jnp.exp(draws), dims[dim] // shards_of).reshape((-1,) + (1,) * (len(dims) - 1 - dim))
    return level


def normal_values(rng, shape, deviation, reach, shards=(), held_as=jnp.bfloat16):
    loudness = shard_levels(rng, shape, shards, -0.22, 0.18) if shards else 1.0
    values = jax.random.normal(rng, shape, jnp.float32) * deviation * loudness
    return jnp.minimum(jnp.maximum(values, -reach), reach).astype(held_as)


def setup_inputs(seed: int = 0) -> dict:
    keys = jax.random.split(jax.random.key(seed), 5)
    factor_window = normal_values(keys[0], (ROWS, COLS), COLS ** -0.5, 0.0625, ((0, 8), (1, 32)))
    upper_panel = normal_values(keys[1], (COLS, PW), 1.0, 6.0, ((0, 32), (1, 8)))
    panel_block = draw_panel_block(jax.random.fold_in(keys[4], 71), 0)
    first_block = draw_first_block(jax.random.fold_in(keys[4], 71), 0)
    return dict(factor_window=factor_window, upper_panel=upper_panel, panel_block=panel_block, first_block=first_block)


def masked_rows(slab_block, slab_start, col_first):
    row_ids = slab_start + jnp.arange(slab_block.shape[0], dtype=jnp.int32)
    inside = (row_ids // BLK)[:, None] >= col_first[None, :]
    return jnp.where(inside, slab_block, jnp.zeros_like(slab_block))


def reference(factor_window, upper_panel, panel_block, first_block):
    col_first = jnp.repeat(first_block, BLK)
    slabs = factor_window.reshape(N_GR, MR_DEV, KC_DEV * N_GC)
    starts = jnp.arange(N_GR, dtype=jnp.int32) * MR_DEV

    def slab_product(slab_item):
        slab_block, slab_start = slab_item
        return jnp.dot(masked_rows(slab_block, slab_start, col_first), upper_panel, preferred_element_type=jnp.float32)

    update = lax.map(slab_product, (slabs, starts)).reshape(N_GR * MR_DEV, PW)
    schur_rows = panel_block - update
    pivot_block = schur_rows[:PW]
    pivot_scale = jnp.mean(jnp.diagonal(pivot_block))
    scaled = pivot_block / pivot_scale
    inverse = jnp.eye(PW, dtype=jnp.float32)
    for iteration in range(NS_ITERS):
        partial_value = jnp.dot(scaled, inverse, precision=lax.Precision.HIGHEST)
        inverse = 2.0 * inverse - jnp.dot(inverse, partial_value, precision=lax.Precision.HIGHEST)
    factor = jnp.dot(schur_rows, inverse, precision=lax.Precision.HIGHEST) / pivot_scale
    return factor.at[:PW].set(inverse)
```

```python
import jax
import jax.numpy as jnp
from jax import lax
from jax.sharding import PartitionSpec as P

BLK = 128
HI = lax.Precision.HIGHEST


def body(factor_window, upper_panel, panel_block, first_block):
    row_groups = lax.axis_size("gr")
    col_groups = lax.axis_size("gc")
    local_rows, local_cols = factor_window.shape
    own_rows = local_rows // col_groups
    width = upper_panel.shape[1] * row_groups
    row_base = lax.axis_index("gr") * local_rows
    col_first = jnp.repeat(first_block, BLK)
    whole_panel = lax.all_gather(upper_panel, "gr", axis=1, tiled=True)
    row_ids = row_base + jnp.arange(local_rows, dtype=jnp.int32)
    masked = jnp.where((row_ids // BLK)[:, None] >= col_first[None, :], factor_window, 0)
    partial = jnp.dot(masked, whole_panel, preferred_element_type=jnp.float32)
    update = lax.psum_scatter(partial, "gc", scatter_dimension=0, tiled=True)
    schur = panel_block - update
    start = (lax.axis_index("gr") * col_groups + lax.axis_index("gc")) * own_rows
    padded = -(-width // own_rows) * own_rows
    spread = jnp.zeros((padded, width), jnp.float32)
    holds = start < width
    at = jnp.where(holds, start, 0)
    spread = lax.dynamic_update_slice(spread, jnp.where(holds, schur, 0.0), (at, 0))[:width]
    piece = lax.psum_scatter(spread, "gc", scatter_dimension=0, tiled=True)
    piece = lax.psum(piece, "gr")
    pivot = lax.all_gather(piece, "gc", axis=0, tiled=True)
    scale = jnp.mean(jnp.diagonal(pivot))
    rows_global = start + jnp.arange(own_rows, dtype=jnp.int32)
    cols = jnp.arange(width, dtype=jnp.int32)
    unit = (rows_global[:, None] == cols[None, :]).astype(jnp.float32)
    left = jnp.where((rows_global < width)[:, None], unit, schur / scale)
    rest = jnp.eye(width, dtype=jnp.float32) - pivot / scale
    square = jnp.dot(rest, rest, precision=HI)
    out = left + jnp.dot(left, rest, precision=HI)
    out = out + jnp.dot(out, square, precision=HI)
    return out + jnp.dot(jnp.dot(out, square, precision=HI), square, precision=HI)


def solution(mesh):
    return jax.shard_map(
        body,
        mesh=mesh,
        in_specs=(P("gr", "gc"), P("gc", "gr"), P(("gr", "gc"), None), P("gc")),
        out_specs=P(("gr", "gc"), None),
        check_vma=False,
    )
```

```python
import jax
import jax.numpy as jnp
from jax import lax
from jax.experimental import pallas as pl
from jax.experimental.pallas import tpu as pltpu
from jax.sharding import PartitionSpec as P

BLK = 128
NX, NC, NY, NZ = 4, 2, 4, 8
PW = 512
ROWS = 104
KC = 256
GW = 64
ROWS_A = 56
POWERS = 7
MESH = pl.DeviceIdType.MESH
F32 = jnp.float32
BF16 = jnp.bfloat16


def split(v):
    hi = v.astype(BF16)
    return hi, (v - hi.astype(F32)).astype(BF16)


def times_transposed(a, bt):
    return lax.dot_general(a, bt, (((1,), (1,)), ((), ())), preferred_element_type=F32)


def kernel(
    window, upper, panel, first, out,
    ut, thr, abuf, mbuf, msend, mrecv, ppan, piece, spread,
    psend, precv, nsend, nrecv,
    loc, uy_s, uy_r, th_s, th_r, ux_s, ux_r, uc_s, uc_r, a_s, a_r, m_s, m_r,
    pan_s, pan_r, mz_s, mz_r, xs_s, xs_r, zs_s, zs_r, ys_s, ys_r, cs_s, cs_r,
    ps_s, ps_r, ns_s, ns_r,
):
    gr, gc = lax.axis_index("gr"), lax.axis_index("gc")
    x, c = gr // NC, gr % NC
    z, y = gc // NY, gc % NY
    pivot_plane = gr == 0
    panel_source = jnp.logical_and(gr == 0, gc < 5)

    def at_y(d):
        return (gr, z * NY + (y + d) % NY)

    def at_z(d):
        return (gr, ((z + d) % NZ) * NY + y)

    def at_x(d):
        return (((x + d) % NX) * NC + c, gc)

    other_core = (x * NC + 1 - c, gc)

    def at_gr(d):
        return ((gr + d) % (NX * NC), gc)

    def remote(src, dst, s, r, who):
        return pltpu.make_async_remote_copy(
            src_ref=src, dst_ref=dst, send_sem=s, recv_sem=r, device_id=who, device_id_type=MESH
        )

    barrier = pltpu.get_barrier_semaphore()
    for d in range(1, NY):
        pl.semaphore_signal(barrier, inc=1, device_id=at_y(d), device_id_type=MESH)
    for d in range(1, NX * NC):
        pl.semaphore_signal(barrier, inc=1, device_id=at_gr(d), device_id_type=MESH)
    for d in range(1, NZ):
        pl.semaphore_signal(barrier, inc=1, device_id=at_z(d), device_id_type=MESH)
    for s in range(2):
        owner = (16 * y + 2 * z + s) // 13

        @pl.when(jnp.logical_and(pivot_plane, owner != gc))
        def _():
            pl.semaphore_signal(barrier, inc=1, device_id=(0, owner), device_id_type=MESH)

    pl.semaphore_wait(barrier, 17 + jnp.where(panel_source, 11 + gc // 4, 0))

    ut[pl.ds(gr * GW, GW), pl.ds(y * KC, KC)] = upper[...]
    lane = lax.broadcasted_iota(jnp.int32, (8, KC), 1)
    thr[:, pl.ds(y * KC, KC)] = jnp.where(lane < BLK, first[0], first[1]) * BLK

    uy = [
        remote(ut.at[pl.ds(gr * GW, GW), pl.ds(y * KC, KC)], ut.at[pl.ds(gr * GW, GW), pl.ds(y * KC, KC)],
               uy_s.at[d - 1], uy_r.at[d - 1], at_y(d))
        for d in range(1, NY)
    ]
    th = [
        remote(thr.at[:, pl.ds(y * KC, KC)], thr.at[:, pl.ds(y * KC, KC)], th_s.at[d - 1], th_r.at[d - 1], at_y(d))
        for d in range(1, NY)
    ]
    for copy in uy + th:
        copy.start()

    mini = [
        remote(window.at[pl.ds(((y + d) % NY) * BLK, BLK), :], mbuf.at[:, pl.ds(y * KC, KC)],
               m_s.at[d - 1], m_r.at[d - 1], at_y(d))
        for d in range(1, NY)
    ]
    mini_own = pltpu.make_async_copy(window.at[pl.ds(y * BLK, BLK), :], mbuf.at[:, pl.ds(y * KC, KC)], loc.at[8])

    @pl.when(pivot_plane)
    def _():
        for copy in mini:
            copy.start()
        mini_own.start()

    order = (4, 3, 5, 2, 6, 1, 7, 0)

    def rows_of(i, yy):
        return pl.ds(pl.multiple_of((((z + order[i]) % NZ) * NY + yy) * ROWS, 8), ROWS)

    exchange, own_rows = [], []
    for i in range(NZ):
        exchange.append([
            remote(window.at[rows_of(i, (y + d) % NY), :], abuf.at[i, :, pl.ds(y * KC, KC)],
                   a_s.at[i, d - 1], a_r.at[i, d - 1], at_y(d))
            for d in range(1, NY)
        ])
        own_rows.append(
            pltpu.make_async_copy(window.at[rows_of(i, y), :], abuf.at[i, :, pl.ds(y * KC, KC)], loc.at[i])
        )
        for copy in exchange[i]:
            copy.start()
        own_rows[i].start()

    def panel_piece(i):
        p = 13 * gc + i
        to = ((p % 16) // 2) * NY + p // 16
        return p, to

    for i in range(13):
        p, to = panel_piece(i)

        @pl.when(jnp.logical_and(jnp.logical_and(panel_source, p < 64), to != gc))
        def _():
            remote(panel.at[pl.ds(8 * i, 8), :], ppan.at[p % 2], pan_s.at[i], pan_r.at[p % 2], (0, to)).start()

        @pl.when(jnp.logical_and(jnp.logical_and(panel_source, p < 64), to == gc))
        def _():
            pltpu.make_async_copy(panel.at[pl.ds(8 * i, 8), :], ppan.at[p % 2], pan_r.at[p % 2]).start()

    def group(d):
        return pl.ds((((x + d) % NX) * NC + c) * GW, GW)

    for copy in uy:
        copy.wait_recv()
    ux = [remote(ut.at[group(0), :], ut.at[group(0), :], ux_s.at[d - 1], ux_r.at[d - 1], at_x(d)) for d in range(1, NX)]
    uc = [remote(ut.at[group(-d), :], ut.at[group(-d), :], uc_s.at[d], uc_r.at[d], other_core) for d in range(NX)]
    for copy in ux:
        copy.start()
    uc[0].start()
    for d in (1, 3, 2):
        ux[d - 1].wait_recv()
        uc[d].start()
    for copy in th:
        copy.wait_recv()
    for copy in uc:
        copy.wait_recv()

    def product(a, row0):
        ids = row0 + lax.broadcasted_iota(jnp.int32, a.shape, 0)
        kept = jnp.where(ids >= thr[0:1, :], a.astype(F32), 0.0).astype(BF16)
        return times_transposed(kept, ut[...])

    mz = [
        remote(msend.at[pl.ds(((z + d) % NZ) * 16, 16), :], mrecv.at[d - 1], mz_s.at[d - 1], mz_r.at[d - 1], at_z(d))
        for d in range(1, NZ)
    ]

    @pl.when(pivot_plane)
    def _():
        mini_own.wait()
        for copy in mini:
            copy.wait_recv()
        msend[...] = product(mbuf[...], y * BLK)
        for copy in mz:
            copy.start()

    def chunk(i):
        own_rows[i].wait()
        for copy in exchange[i]:
            copy.wait_recv()
        return product(abuf[i], gr * (ROWS * NY * NZ) + (((z + order[i]) % NZ) * NY + y) * ROWS)

    parts = (pl.ds(0, ROWS_A), pl.ds(ROWS_A, ROWS - ROWS_A))

    def ring(send, recv, s, r, step):
        return [
            [remote(send.at[k, part, :], recv.at[k, part, :], s.at[k, h], r.at[k, h], at_z(step)) for h, part in enumerate(parts)]
            for k in range(4)
        ]

    plus, minus = ring(psend, precv, ps_s, ps_r, 1), ring(nsend, nrecv, ns_s, ns_r, NZ - 1)

    def first_chunk():
        v = chunk(0)
        psend[0, parts[0], :] = v[:ROWS_A]
        plus[0][0].start()
        nsend[0, parts[1], :] = v[ROWS_A:]
        minus[0][1].start()

    def next_chunk(i, k, ring_, send, recv, came):
        send[k] = chunk(i)
        for h in range(2):
            if h not in came:
                ring_[k][h].start()
        for h in came:
            ring_[k - 1][h].wait_recv()
            send[k, parts[h], :] += recv[k - 1, parts[h], :]
            ring_[k][h].start()

    first_chunk()
    next_chunk(1, 1, plus, psend, precv, (0,))
    next_chunk(2, 1, minus, nsend, nrecv, (1,))

    spread_x = [
        remote(piece.at[(d % NC)], spread.at[y, z, d % NC], xs_s.at[d - 1], xs_r.at[0], (d, gc))
        for d in range(1, NX * NC)
    ]

    @pl.when(pivot_plane)
    def _():
        for copy in mz:
            copy.wait_recv()
        total = msend[pl.ds(z * 16, 16), :]
        for d in range(1, NZ):
            total = total + mrecv[d - 1]
        for s in range(2):
            pltpu.make_async_copy(panel.at[pl.ds(0, 8), :], ppan.at[s], pan_r.at[s]).wait()
            piece[s] = ppan[s] - total[8 * s : 8 * s + 8]
        spread[y, z, 0] = piece[0]
        for copy in spread_x:
            copy.start()

    @pl.when(jnp.logical_not(pivot_plane))
    def _():
        remote(piece.at[0], spread.at[y, z, c], xs_s.at[0], xs_r.at[0], (0, gc)).wait_recv()

    spread_z = [
        remote(spread.at[y, z, c], spread.at[y, z, c], zs_s.at[d - 1], zs_r.at[d - 1], at_z(d)) for d in range(1, NZ)
    ]
    for copy in spread_z:
        copy.start()

    next_chunk(3, 2, plus, psend, precv, (0, 1))
    next_chunk(4, 2, minus, nsend, nrecv, (1, 0))

    for copy in spread_z:
        copy.wait_recv()
    spread_y = [
        remote(spread.at[y, :, c], spread.at[y, :, c], ys_s.at[d - 1], ys_r.at[d - 1], at_y(d)) for d in range(1, NY)
    ]
    spread_c = [
        remote(spread.at[(y + NY - d) % NY, :, c], spread.at[(y + NY - d) % NY, :, c], cs_s.at[d], cs_r.at[d], other_core)
        for d in range(NY)
    ]
    for copy in spread_y:
        copy.start()
    spread_c[0].start()

    next_chunk(5, 3, plus, psend, precv, (0, 1))
    next_chunk(6, 3, minus, nsend, nrecv, (1, 0))
    update = chunk(7)
    for h in range(2):
        plus[3][h].wait_recv()
        minus[3][h].wait_recv()
    schur = panel[...] - (update + precv[3] + nrecv[3])

    for d in (1, 3, 2):
        spread_y[d - 1].wait_recv()
        spread_c[d].start()
    for copy in spread_c:
        copy.wait_recv()

    pivot = spread[...].reshape(PW, PW)
    same = lax.broadcasted_iota(jnp.int32, (PW, PW), 0) == lax.broadcasted_iota(jnp.int32, (PW, PW), 1)
    scale = jnp.sum(jnp.sum(jnp.where(same, pivot, 0.0), axis=0, keepdims=True), axis=1, keepdims=True) / PW
    rest_hi, rest_lo = split(jnp.where(same, 1.0, 0.0) - pivot / scale)
    row_ids = (gr * NY * NZ + gc) * ROWS + lax.broadcasted_iota(jnp.int32, (ROWS, PW), 0)
    unit = jnp.where(row_ids == lax.broadcasted_iota(jnp.int32, (ROWS, PW), 1), 1.0, 0.0)
    left = jnp.where(row_ids < PW, unit, schur / scale)
    total = left
    for _ in range(POWERS):
        hi, lo = split(total)
        total = left + (
            jnp.dot(hi, rest_hi, preferred_element_type=F32)
            + (jnp.dot(hi, rest_lo, preferred_element_type=F32) + jnp.dot(lo, rest_hi, preferred_element_type=F32))
        )
    out[...] = total

    for copy in uy + th + ux + uc + spread_z + spread_y + spread_c:
        copy.wait_send()
    for copies in exchange:
        for copy in copies:
            copy.wait_send()
    plus[0][0].wait_send()
    minus[0][1].wait_send()
    for k in range(1, 4):
        for h in range(2):
            plus[k][h].wait_send()
            minus[k][h].wait_send()

    @pl.when(pivot_plane)
    def _():
        for copy in mini + mz + spread_x:
            copy.wait_send()

    for i in range(13):
        p, to = panel_piece(i)

        @pl.when(jnp.logical_and(jnp.logical_and(panel_source, p < 64), to != gc))
        def _():
            remote(panel.at[pl.ds(8 * i, 8), :], ppan.at[p % 2], pan_s.at[i], pan_r.at[p % 2], (0, to)).wait_send()


def body(window, upper, panel, first):
    vmem, dma = pltpu.VMEM, pltpu.SemaphoreType.DMA
    spec = pl.BlockSpec(memory_space=pltpu.VMEM)

    def both(*shape):
        return [dma(shape), dma(shape)]

    return pl.pallas_call(
        kernel,
        out_shape=jax.ShapeDtypeStruct((ROWS, PW), F32),
        in_specs=[pl.BlockSpec(memory_space=pl.ANY), spec, spec, pl.BlockSpec(memory_space=pltpu.SMEM)],
        out_specs=spec,
        scratch_shapes=[
            vmem((PW, NY * KC), BF16),
            vmem((8, NY * KC), jnp.int32),
            vmem((NZ, ROWS, NY * KC), BF16),
            vmem((BLK, NY * KC), BF16),
            vmem((BLK, PW), F32),
            vmem((NZ - 1, 16, PW), F32),
            vmem((2, 8, PW), F32),
            vmem((2, 8, PW), F32),
            vmem((NY, NZ, NC, 8, PW), F32),
            *[vmem((4, ROWS, PW), F32) for _ in range(4)],
            dma((9,)),
            *both(NY - 1), *both(NY - 1), *both(NX - 1), *both(NX), *both(NZ, NY - 1), *both(NY - 1),
            dma((13,)), dma((2,)), *both(NZ - 1), dma((NX * NC - 1,)), dma((1,)),
            *both(NZ - 1), *both(NY - 1), *both(NY), *both(4, 2), *both(4, 2),
        ],
        compiler_params=pltpu.CompilerParams(
            collective_id=0, has_side_effects=True, vmem_limit_bytes=60 * 1024 * 1024
        ),
        name="panel_update",
    )(window, upper.T, panel, first)


def solution(mesh):
    return jax.shard_map(
        body,
        mesh=mesh,
        in_specs=(P("gr", "gc"), P("gc", "gr"), P(("gr", "gc"), None), P("gc")),
        out_specs=P(("gr", "gc"), None),
        check_vma=False,
    )
```

```python
import jax
import jax.numpy as jnp
from jax import lax
from jax.experimental import pallas as pl
from jax.experimental.pallas import tpu as pltpu
from jax.sharding import PartitionSpec as P

BLK = 128
NX, NC, NY, NZ = 4, 2, 4, 8
PW = 512
ROWS = 104
KC = 256
GW = 64
ROWS_A = 56
POWERS = 7
MESH = pl.DeviceIdType.MESH
F32 = jnp.float32
BF16 = jnp.bfloat16


def split(v):
    hi = v.astype(BF16)
    return hi, (v - hi.astype(F32)).astype(BF16)


def times_transposed(a, bt):
    return lax.dot_general(a, bt, (((1,), (1,)), ((), ())), preferred_element_type=F32)


def kernel(
    window, upper, panel, first, out,
    ut, thr, pown, abuf, mbuf, msend, mrecv, ppan, piece, spread,
    psend, precv, nsend, nrecv,
    loc, sent, uy_r, th_r, ux_r, uc_r, a_r, m_r, pan_r, mz_r, xs_r, zs_r, ys_r, cs_r, ps_r, ns_r,
):
    gr, gc = lax.axis_index("gr"), lax.axis_index("gc")
    x, c = gr // NC, gr % NC
    z, y = gc // NY, gc % NY
    pivot_plane = gr == 0
    panel_source = jnp.logical_and(gr == 0, gc < 5)

    def at_y(d):
        return (gr, z * NY + (y + d) % NY)

    def at_z(d):
        return (gr, ((z + d) % NZ) * NY + y)

    def at_x(d):
        return (((x + d) % NX) * NC + c, gc)

    other_core = (x * NC + 1 - c, gc)

    def at_gr(d):
        return ((gr + d) % (NX * NC), gc)

    def remote(src, dst, s, r, who):
        return pltpu.make_async_remote_copy(
            src_ref=src, dst_ref=dst, send_sem=s, recv_sem=r, device_id=who, device_id_type=MESH
        )

    def arrived(like, sem):
        pltpu.make_async_copy(like, like, sem).wait()

    barrier = pltpu.get_barrier_semaphore()
    for d in range(1, NY):
        pl.semaphore_signal(barrier, inc=1, device_id=at_y(d), device_id_type=MESH)
    for d in range(1, NX * NC):
        pl.semaphore_signal(barrier, inc=1, device_id=at_gr(d), device_id_type=MESH)
    for d in range(1, NZ):
        pl.semaphore_signal(barrier, inc=1, device_id=at_z(d), device_id_type=MESH)
    for s in range(2):
        owner = (16 * y + 2 * z + s) // 13

        @pl.when(jnp.logical_and(pivot_plane, owner != gc))
        def _():
            pl.semaphore_signal(barrier, inc=1, device_id=(0, owner), device_id_type=MESH)

    pl.semaphore_wait(barrier, 17 + jnp.where(panel_source, 11 + gc // 4, 0))

    def group(d):
        return pl.ds((((x + d) % NX) * NC + c) * GW, GW)

    def cols(d):
        return pl.ds(((y + d) % NY) * KC, KC)

    lane = lax.broadcasted_iota(jnp.int32, (8, KC), 1)
    thr[:, pl.ds(y * KC, KC)] = jnp.where(lane < BLK, first[0], first[1]) * BLK
    uy = [remote(upper, ut.at[group(0), cols(0)], sent.at[0], uy_r.at[d - 1], at_y(d)) for d in range(1, NY)]
    th = [
        remote(thr.at[:, cols(0)], thr.at[:, cols(0)], sent.at[1], th_r, at_y(d)) for d in range(1, NY)
    ]
    ux = [
        [
            remote(ut.at[group(0), cols(-j)] if j else upper, ut.at[group(0), cols(-j)],
                   sent.at[2], ux_r.at[d - 1], at_x(d))
            for j in range(NY)
        ]
        for d in range(1, NX)
    ]
    upper_own = pltpu.make_async_copy(upper, ut.at[group(0), cols(0)], loc.at[0])
    panel_own = pltpu.make_async_copy(panel, pown, loc.at[1])
    for d in (1, 3, 2):
        uy[d - 1].start()
    for d in (1, 3, 2):
        ux[d - 1][0].start()
    for copy in th:
        copy.start()
    upper_own.start()

    mini = [
        remote(window.at[pl.ds(((y + d) % NY) * BLK, BLK), :], mbuf.at[:, pl.ds(y * KC, KC)],
               sent.at[4], m_r, at_y(d))
        for d in range(1, NY)
    ]
    mini_own = pltpu.make_async_copy(window.at[pl.ds(y * BLK, BLK), :], mbuf.at[:, pl.ds(y * KC, KC)], m_r)

    @pl.when(pivot_plane)
    def _():
        for copy in mini:
            copy.start()
        mini_own.start()

    order = (4, 3, 5, 2, 6, 1, 7, 0)

    def rows_of(i, yy):
        return pl.ds(pl.multiple_of((((z + order[i]) % NZ) * NY + yy) * ROWS, 8), ROWS)

    exchange, own_rows = [], []
    for i in range(NZ):
        exchange.append([
            remote(window.at[rows_of(i, (y + d) % NY), :], abuf.at[i, :, pl.ds(y * KC, KC)],
                   sent.at[5], a_r.at[i], at_y(d))
            for d in range(1, NY)
        ])
        own_rows.append(
            pltpu.make_async_copy(window.at[rows_of(i, y), :], abuf.at[i, :, pl.ds(y * KC, KC)], a_r.at[i])
        )
        for copy in exchange[i]:
            copy.start()
        own_rows[i].start()

    panel_own.start()

    def panel_piece(i):
        p = 13 * gc + i
        to = ((p % 16) // 2) * NY + p // 16
        return p, to

    for i in range(13):
        p, to = panel_piece(i)

        @pl.when(jnp.logical_and(jnp.logical_and(panel_source, p < 64), to != gc))
        def _():
            remote(panel.at[pl.ds(8 * i, 8), :], ppan.at[p % 2], sent.at[6], pan_r, (0, to)).start()

        @pl.when(jnp.logical_and(jnp.logical_and(panel_source, p < 64), to == gc))
        def _():
            pltpu.make_async_copy(panel.at[pl.ds(8 * i, 8), :], ppan.at[p % 2], pan_r).start()

    for j in (1, 3, 2):
        uy[j - 1].wait_recv()
        for d in (1, 3, 2):
            ux[d - 1][j].start()
    uc = [remote(ut.at[group(-d), :], ut.at[group(-d), :], sent.at[3], uc_r, other_core) for d in range(NX)]
    upper_own.wait()
    uc[0].start()
    for d in (1, 3, 2):
        arrived(ut.at[group(-d), :], ux_r.at[d - 1])
        uc[d].start()
    arrived(thr.at[:, pl.ds(0, (NY - 1) * KC)], th_r)
    arrived(ut.at[pl.ds(0, PW // NC), :], uc_r)

    def product(a, row0):
        ids = row0 + lax.broadcasted_iota(jnp.int32, a.shape, 0)
        kept = jnp.where(ids >= thr[0:1, :], a.astype(F32), 0.0).astype(BF16)
        return times_transposed(kept, ut[...])

    mz = [
        remote(msend.at[pl.ds(((z + d) % NZ) * 16, 16), :], mrecv.at[d - 1], sent.at[7], mz_r, at_z(d))
        for d in range(1, NZ)
    ]

    @pl.when(pivot_plane)
    def _():
        arrived(mbuf, m_r)
        msend[...] = product(mbuf[...], y * BLK)
        for copy in mz:
            copy.start()

    def chunk(i):
        arrived(abuf.at[i], a_r.at[i])
        return product(abuf[i], gr * (ROWS * NY * NZ) + (((z + order[i]) % NZ) * NY + y) * ROWS)

    parts = (pl.ds(0, ROWS_A), pl.ds(ROWS_A, ROWS - ROWS_A))

    def ring(send, recv, r, step):
        return [
            [remote(send.at[k, part, :], recv.at[k, part, :], sent.at[8], r.at[k, h], at_z(step)) for h, part in enumerate(parts)]
            for k in range(4)
        ]

    plus, minus = ring(psend, precv, ps_r, 1), ring(nsend, nrecv, ns_r, NZ - 1)

    def forward(k, h):
        plus[k - 1][h].wait_recv()
        psend[k, parts[h], :] += precv[k - 1, parts[h], :]
        plus[k][h].start()
        minus[k - 1][1 - h].wait_recv()
        nsend[k, parts[1 - h], :] += nrecv[k - 1, parts[1 - h], :]
        minus[k][1 - h].start()

    update = chunk(0)
    psend[0, parts[0], :] = update[:ROWS_A]
    plus[0][0].start()
    nsend[0, parts[1], :] = update[ROWS_A:]
    minus[0][1].start()
    psend[1] = chunk(1)
    plus[1][1].start()
    spread_x = [
        remote(piece.at[(d % NC)], spread.at[y, z, d % NC], sent.at[9], xs_r, (d, gc))
        for d in range(1, NX * NC)
    ]

    spread_z = [
        remote(spread.at[y, z, c], spread.at[y, z, c], sent.at[10], zs_r.at[d - 1], at_z(d)) for d in range(1, NZ)
    ]
    spread_y = [
        [
            remote(spread.at[y, (z + NZ - j) % NZ, c], spread.at[y, (z + NZ - j) % NZ, c],
                   sent.at[11], ys_r.at[d - 1], at_y(d))
            for j in range(NZ)
        ]
        for d in range(1, NY)
    ]

    def spread_own():
        for d in (4, 3, 5, 2, 6, 1, 7):
            spread_z[d - 1].start()
        for d in (1, 3, 2):
            spread_y[d - 1][0].start()

    @pl.when(pivot_plane)
    def _():
        arrived(mrecv, mz_r)
        arrived(ppan, pan_r)
        total = msend[pl.ds(z * 16, 16), :]
        for d in range(1, NZ):
            total = total + mrecv[d - 1]
        for s in range(2):
            piece[s] = ppan[s] - total[8 * s : 8 * s + 8]
        spread[y, z, 0] = piece[0]
        for copy in spread_x:
            copy.start()
        spread_own()

    nsend[1] = chunk(2)
    minus[1][0].start()
    forward(1, 0)
    psend[2] = chunk(3)
    nsend[2] = chunk(4)
    forward(2, 1)

    forward(2, 0)

    @pl.when(jnp.logical_not(pivot_plane))
    def _():
        remote(piece.at[0], spread.at[y, z, c], sent.at[9], xs_r, (0, gc)).wait_recv()
        spread_own()


    psend[3] = chunk(5)
    nsend[3] = chunk(6)
    forward(3, 1)
    forward(3, 0)

    for j in (1, 7, 2, 6, 3, 5, 4):
        spread_z[j - 1].wait_recv()
        for d in (1, 3, 2):
            spread_y[d - 1][j].start()
    spread_c = [
        remote(spread.at[(y + NY - d) % NY, :, c], spread.at[(y + NY - d) % NY, :, c], sent.at[12], cs_r, other_core)
        for d in range(NY)
    ]
    spread_c[0].start()

    update = chunk(7)
    panel_own.wait()
    for h in (1, 0):
        plus[3][h].wait_recv()
        minus[3][1 - h].wait_recv()
    schur = pown[...] - (update + precv[3] + nrecv[3])

    for d in (1, 3, 2):
        arrived(spread.at[0, :, 0], ys_r.at[d - 1])
        spread_c[d].start()
    arrived(spread.at[:, :, 0], cs_r)

    pivot = spread[...].reshape(PW, PW)
    same = lax.broadcasted_iota(jnp.int32, (PW, PW), 0) == lax.broadcasted_iota(jnp.int32, (PW, PW), 1)
    scale = jnp.sum(jnp.sum(jnp.where(same, pivot, 0.0), axis=0, keepdims=True), axis=1, keepdims=True) / PW
    rest_hi, rest_lo = split(jnp.where(same, 1.0, 0.0) - pivot / scale)
    row_ids = (gr * NY * NZ + gc) * ROWS + lax.broadcasted_iota(jnp.int32, (ROWS, PW), 0)
    unit = jnp.where(row_ids == lax.broadcasted_iota(jnp.int32, (ROWS, PW), 1), 1.0, 0.0)
    left = jnp.where(row_ids < PW, unit, schur / scale)
    total = left
    for _ in range(POWERS):
        hi, lo = split(total)
        both = jnp.dot(jnp.concatenate([hi, lo]), rest_hi, preferred_element_type=F32)
        total = left + (both[:ROWS] + (both[ROWS:] + jnp.dot(hi, rest_lo, preferred_element_type=F32)))
    out[...] = total

    arrived(ut.at[pl.ds(0, 48), :], sent.at[0])
    arrived(thr.at[:, pl.ds(0, (NY - 1) * KC)], sent.at[1])
    arrived(ut.at[pl.ds(0, 3 * GW), :], sent.at[2])
    arrived(ut.at[pl.ds(0, PW // NC), :], sent.at[3])
    arrived(abuf.at[:, :, pl.ds(0, (NY - 1) * KC)], sent.at[5])
    arrived(abuf.at[:, :, pl.ds(0, 7 * BLK)], sent.at[8])
    arrived(spread.at[0, pl.ds(0, NZ - 1), 0], sent.at[10])
    arrived(spread.at[pl.ds(0, NY - 1), :, 0], sent.at[11])
    arrived(spread.at[:, :, 0], sent.at[12])

    @pl.when(pivot_plane)
    def _():
        arrived(mbuf.at[:, pl.ds(0, (NY - 1) * KC)], sent.at[4])
        arrived(mrecv, sent.at[7])
        arrived(spread.at[0, pl.ds(0, NZ - 1), 0], sent.at[9])

    @pl.when(jnp.logical_and(gr == 0, gc < 4))
    def _():
        arrived(panel.at[pl.ds(0, 88), :], sent.at[6])

    @pl.when(jnp.logical_and(gr == 0, gc == 4))
    def _():
        arrived(panel.at[pl.ds(0, 96), :], sent.at[6])


def body(window, upper, panel, first):
    vmem, dma = pltpu.VMEM, pltpu.SemaphoreType.DMA
    spec = pl.BlockSpec(memory_space=pltpu.VMEM)

    return pl.pallas_call(
        kernel,
        out_shape=jax.ShapeDtypeStruct((ROWS, PW), F32),
        in_specs=[*[pl.BlockSpec(memory_space=pl.ANY)] * 3, pl.BlockSpec(memory_space=pltpu.SMEM)],
        out_specs=spec,
        scratch_shapes=[
            vmem((PW, NY * KC), BF16),
            vmem((8, NY * KC), jnp.int32),
            vmem((ROWS, PW), F32),
            vmem((NZ, ROWS, NY * KC), BF16),
            vmem((BLK, NY * KC), BF16),
            vmem((BLK, PW), F32),
            vmem((NZ - 1, 16, PW), F32),
            vmem((2, 8, PW), F32),
            vmem((2, 8, PW), F32),
            vmem((NY, NZ, NC, 8, PW), F32),
            *[vmem((4, ROWS, PW), F32) for _ in range(4)],
            dma((2,)), dma((13,)),
            dma((NY - 1,)), dma, dma((NX - 1,)), dma, dma((NZ,)), dma, dma, dma, dma,
            dma((NZ - 1,)), dma((NY - 1,)), dma, dma((4, 2)), dma((4, 2)),
        ],
        compiler_params=pltpu.CompilerParams(
            collective_id=0, has_side_effects=True, vmem_limit_bytes=63 * 1024 * 1024
        ),
        name="panel_update",
    )(window, upper.T, panel, first)


def solution(mesh):
    return jax.shard_map(
        body,
        mesh=mesh,
        in_specs=(P("gr", "gc"), P("gc", "gr"), P(("gr", "gc"), None), P("gc")),
        out_specs=P(("gr", "gc"), None),
        check_vma=False,
    )
```

```python
import jax
import jax.numpy as jnp
from jax import lax
from jax.experimental import pallas as pl
from jax.experimental.pallas import tpu as pltpu
from jax.sharding import PartitionSpec as P

BLK = 128
NX, NC, NY, NZ = 4, 2, 4, 8
PW = 512
ROWS = 104
KC = 256
GW = 64
PARTS = (56, 48)
LEVELS = 32767.0
POWERS = 7
MESH = pl.DeviceIdType.MESH
F32 = jnp.float32
BF16 = jnp.bfloat16


def split(v):
    hi = v.astype(BF16)
    return hi, (v - hi.astype(F32)).astype(BF16)


def coded(v):
    step = jnp.maximum(jnp.max(jnp.abs(v), axis=0, keepdims=True) * (1.0 / LEVELS), 1e-37)
    return jnp.round(v * (1.0 / step)).astype(jnp.int32).astype(jnp.int16), step


def times_transposed(a, bt):
    return lax.dot_general(a, bt, (((1,), (1,)), ((), ())), preferred_element_type=F32)


def kernel(
    window, upper, panel, first_block, out,
    first, ut, thr, pown, abuf, mbuf, msend, mrecv, ppan, piece, spread,
    sums, codes, steps,
    loc, sent, uy_r, th_r, ux_r, uc_r, a_r, m_r, pan_r, mz_r, xs_r, zs_r, ys_r, cs_r, ring_r,
):
    gr, gc = lax.axis_index("gr"), lax.axis_index("gc")
    x, c = gr // NC, gr % NC
    z, y = gc // NY, gc % NY
    pivot_plane = gr == 0
    panel_source = jnp.logical_and(gr == 0, gc < 5)

    def at_y(d):
        return (gr, z * NY + (y + d) % NY)

    def at_z(d):
        return (gr, ((z + d) % NZ) * NY + y)

    def at_x(d):
        return (((x + d) % NX) * NC + c, gc)

    other_core = (x * NC + 1 - c, gc)

    def at_gr(d):
        return ((gr + d) % (NX * NC), gc)

    def remote(src, dst, s, r, who):
        return pltpu.make_async_remote_copy(
            src_ref=src, dst_ref=dst, send_sem=s, recv_sem=r, device_id=who, device_id_type=MESH
        )

    def arrived(like, sem):
        pltpu.make_async_copy(like, like, sem).wait()

    first_own = pltpu.make_async_copy(first_block, first, loc.at[2])
    first_own.start()

    barrier = pltpu.get_barrier_semaphore()
    for d in range(1, NY):
        pl.semaphore_signal(barrier, inc=1, device_id=at_y(d), device_id_type=MESH)
    for d in range(1, NX * NC):
        pl.semaphore_signal(barrier, inc=1, device_id=at_gr(d), device_id_type=MESH)
    for d in range(1, NZ):
        pl.semaphore_signal(barrier, inc=1, device_id=at_z(d), device_id_type=MESH)
    for s in range(2):
        owner = (16 * y + 2 * z + s) // 13

        @pl.when(jnp.logical_and(pivot_plane, owner != gc))
        def _():
            pl.semaphore_signal(barrier, inc=1, device_id=(0, owner), device_id_type=MESH)

    pl.semaphore_wait(barrier, 17 + jnp.where(panel_source, 11 + gc // 4, 0))

    def group(d):
        return pl.ds((((x + d) % NX) * NC + c) * GW, GW)

    def cols(d):
        return pl.ds(((y + d) % NY) * KC, KC)

    lane = lax.broadcasted_iota(jnp.int32, (8, KC), 1)
    first_own.wait()
    thr[:, pl.ds(y * KC, KC)] = jnp.where(lane < BLK, first[0], first[1]) * BLK
    uy = [remote(upper, ut.at[group(0), cols(0)], sent.at[0], uy_r.at[d - 1], at_y(d)) for d in range(1, NY)]
    th = [
        remote(thr.at[:, cols(0)], thr.at[:, cols(0)], sent.at[1], th_r, at_y(d)) for d in range(1, NY)
    ]
    ux = [
        [
            remote(ut.at[group(0), cols(-j)] if j else upper, ut.at[group(0), cols(-j)],
                   sent.at[2], ux_r.at[d - 1], at_x(d))
            for j in range(NY)
        ]
        for d in range(1, NX)
    ]
    upper_own = pltpu.make_async_copy(upper, ut.at[group(0), cols(0)], loc.at[0])
    panel_own = pltpu.make_async_copy(panel, pown, loc.at[1])
    for d in (1, 3, 2):
        uy[d - 1].start()
    for d in (1, 3, 2):
        ux[d - 1][0].start()
    for copy in th:
        copy.start()
    upper_own.start()

    mini = [
        remote(window.at[pl.ds(((y + d) % NY) * BLK, BLK), :], mbuf.at[:, pl.ds(y * KC, KC)],
               sent.at[4], m_r, at_y(d))
        for d in range(1, NY)
    ]
    mini_own = pltpu.make_async_copy(window.at[pl.ds(y * BLK, BLK), :], mbuf.at[:, pl.ds(y * KC, KC)], m_r)

    @pl.when(pivot_plane)
    def _():
        for copy in mini:
            copy.start()
        mini_own.start()

    order = (4, 3, 5, 2, 6, 1, 7, 0)

    def rows_of(i, yy):
        return pl.ds(pl.multiple_of((((z + order[i]) % NZ) * NY + yy) * ROWS, 8), ROWS)

    exchange, own_rows = [], []
    for i in range(NZ):
        exchange.append([
            remote(window.at[rows_of(i, (y + d) % NY), :], abuf.at[i, :, pl.ds(y * KC, KC)],
                   sent.at[5], a_r.at[i], at_y(d))
            for d in range(1, NY)
        ])
        own_rows.append(
            pltpu.make_async_copy(window.at[rows_of(i, y), :], abuf.at[i, :, pl.ds(y * KC, KC)], a_r.at[i])
        )
        for copy in exchange[i]:
            copy.start()
        own_rows[i].start()

    panel_own.start()

    def panel_piece(i):
        p = 13 * gc + i
        to = ((p % 16) // 2) * NY + p // 16
        return p, to

    for i in range(13):
        p, to = panel_piece(i)

        @pl.when(jnp.logical_and(jnp.logical_and(panel_source, p < 64), to != gc))
        def _():
            remote(panel.at[pl.ds(8 * i, 8), :], ppan.at[p % 2], sent.at[6], pan_r, (0, to)).start()

        @pl.when(jnp.logical_and(jnp.logical_and(panel_source, p < 64), to == gc))
        def _():
            pltpu.make_async_copy(panel.at[pl.ds(8 * i, 8), :], ppan.at[p % 2], pan_r).start()

    for j in (1, 3, 2):
        uy[j - 1].wait_recv()
        for d in (1, 3, 2):
            ux[d - 1][j].start()
    uc = [remote(ut.at[group(-d), :], ut.at[group(-d), :], sent.at[3], uc_r, other_core) for d in range(NX)]
    upper_own.wait()
    uc[0].start()
    for d in (1, 3, 2):
        arrived(ut.at[group(-d), :], ux_r.at[d - 1])
        uc[d].start()
    arrived(thr.at[:, pl.ds(0, (NY - 1) * KC)], th_r)
    arrived(ut.at[pl.ds(0, PW // NC), :], uc_r)

    def product(a, row0):
        ids = row0 + lax.broadcasted_iota(jnp.int32, a.shape, 0)
        kept = jnp.where(ids >= thr[0:1, :], a.astype(F32), 0.0).astype(BF16)
        return times_transposed(kept, ut[...])

    mz = [
        remote(msend.at[pl.ds(((z + d) % NZ) * 16, 16), :], mrecv.at[d - 1], sent.at[7], mz_r, at_z(d))
        for d in range(1, NZ)
    ]

    @pl.when(pivot_plane)
    def _():
        arrived(mbuf, m_r)
        msend[...] = product(mbuf[...], y * BLK)
        for copy in mz:
            copy.start()

    def chunk(i):
        arrived(abuf.at[i], a_r.at[i])
        return product(abuf[i], gr * (ROWS * NY * NZ) + (((z + order[i]) % NZ) * NY + y) * ROWS)

    parts = (pl.ds(0, PARTS[0]), pl.ds(PARTS[0], PARTS[1]))
    PLUS, MINUS = 0, 1
    hops = (at_z(1), at_z(NZ - 1))

    def message(way, k, h):
        at = 16 * way + 2 * k + h
        rows = pl.ds(0, PARTS[h])
        return [
            remote(codes.at[at, rows, :], codes.at[at + 8, rows, :], sent.at[8], ring_r.at[way, k, h], hops[way]),
            remote(steps.at[at], steps.at[at + 8], sent.at[13], ring_r.at[way, k, h], hops[way]),
        ]

    def send_on(way, k, h, v):
        at = 16 * way + 2 * k + h
        codes[at, pl.ds(0, PARTS[h]), :], steps[at] = coded(v)
        for copy in message(way, k, h):
            copy.start()

    def came(way, k, h):
        at = 16 * way + 2 * k + h + 8
        arrived(steps.at[pl.ds(0, PARTS[h] // 2 + 1)], ring_r.at[way, k, h])
        return codes[at, pl.ds(0, PARTS[h]), :].astype(jnp.int32).astype(F32) * steps[at]

    def forward(k, h):
        send_on(PLUS, k, h, sums[2 * k - 1, parts[h], :] + came(PLUS, k - 1, h))
        send_on(MINUS, k, 1 - h, sums[2 * k, parts[1 - h], :] + came(MINUS, k - 1, 1 - h))

    update = chunk(0)
    send_on(PLUS, 0, 0, update[: PARTS[0]])
    send_on(MINUS, 0, 1, update[PARTS[0] :])
    sums[1] = chunk(1)
    send_on(PLUS, 1, 1, sums[1, parts[1], :])
    spread_x = [
        remote(piece.at[(d % NC)], spread.at[y, z, d % NC], sent.at[9], xs_r, (d, gc))
        for d in range(1, NX * NC)
    ]

    spread_z = [
        remote(spread.at[y, z, c], spread.at[y, z, c], sent.at[10], zs_r.at[d - 1], at_z(d)) for d in range(1, NZ)
    ]
    spread_y = [
        [
            remote(spread.at[y, (z + NZ - j) % NZ, c], spread.at[y, (z + NZ - j) % NZ, c],
                   sent.at[11], ys_r.at[d - 1], at_y(d))
            for j in range(NZ)
        ]
        for d in range(1, NY)
    ]

    def spread_own():
        for d in (4, 3, 5, 2, 6, 1, 7):
            spread_z[d - 1].start()
        for d in (1, 3, 2):
            spread_y[d - 1][0].start()

    @pl.when(pivot_plane)
    def _():
        arrived(mrecv, mz_r)
        arrived(ppan, pan_r)
        total = msend[pl.ds(z * 16, 16), :]
        for d in range(1, NZ):
            total = total + mrecv[d - 1]
        for s in range(2):
            piece[s] = ppan[s] - total[8 * s : 8 * s + 8]
        spread[y, z, 0] = piece[0]
        for copy in spread_x:
            copy.start()
        spread_own()

    sums[2] = chunk(2)
    send_on(MINUS, 1, 0, sums[2, parts[0], :])
    forward(1, 0)
    sums[3] = chunk(3)
    sums[4] = chunk(4)
    forward(2, 1)

    forward(2, 0)

    @pl.when(jnp.logical_not(pivot_plane))
    def _():
        remote(piece.at[0], spread.at[y, z, c], sent.at[9], xs_r, (0, gc)).wait_recv()
        spread_own()


    sums[5] = chunk(5)
    sums[6] = chunk(6)
    forward(3, 1)
    forward(3, 0)

    for j in (1, 7, 2, 6, 3, 5, 4):
        spread_z[j - 1].wait_recv()
        for d in (1, 3, 2):
            spread_y[d - 1][j].start()
    spread_c = [
        remote(spread.at[(y + NY - d) % NY, :, c], spread.at[(y + NY - d) % NY, :, c], sent.at[12], cs_r, other_core)
        for d in range(NY)
    ]
    spread_c[0].start()

    sums[0] = chunk(7)
    panel_own.wait()
    for h in (1, 0):
        sums[0, parts[h], :] += came(PLUS, 3, h)
        sums[0, parts[1 - h], :] += came(MINUS, 3, 1 - h)
    schur = pown[...] - sums[0]

    for d in (1, 3, 2):
        arrived(spread.at[0, :, 0], ys_r.at[d - 1])
        spread_c[d].start()
    arrived(spread.at[:, :, 0], cs_r)

    pivot = spread[...].reshape(PW, PW)
    same = lax.broadcasted_iota(jnp.int32, (PW, PW), 0) == lax.broadcasted_iota(jnp.int32, (PW, PW), 1)
    scale = jnp.sum(jnp.sum(jnp.where(same, pivot, 0.0), axis=0, keepdims=True), axis=1, keepdims=True) / PW
    rest_hi, rest_lo = split(jnp.where(same, 1.0, 0.0) - pivot / scale)
    row_ids = (gr * NY * NZ + gc) * ROWS + lax.broadcasted_iota(jnp.int32, (ROWS, PW), 0)
    unit = jnp.where(row_ids == lax.broadcasted_iota(jnp.int32, (ROWS, PW), 1), 1.0, 0.0)
    left = jnp.where(row_ids < PW, unit, schur / scale)
    total = left
    for _ in range(POWERS):
        hi, lo = split(total)
        both = jnp.dot(jnp.concatenate([hi, lo]), rest_hi, preferred_element_type=F32)
        total = left + (both[:ROWS] + (both[ROWS:] + jnp.dot(hi, rest_lo, preferred_element_type=F32)))
    out[...] = total

    arrived(ut.at[pl.ds(0, 48), :], sent.at[0])
    arrived(thr.at[:, pl.ds(0, (NY - 1) * KC)], sent.at[1])
    arrived(ut.at[pl.ds(0, 3 * GW), :], sent.at[2])
    arrived(ut.at[pl.ds(0, PW // NC), :], sent.at[3])
    arrived(abuf.at[:, :, pl.ds(0, (NY - 1) * KC)], sent.at[5])
    arrived(codes.at[pl.ds(0, 13)], sent.at[8])
    arrived(steps.at[pl.ds(0, 14)], sent.at[13])
    arrived(spread.at[0, pl.ds(0, NZ - 1), 0], sent.at[10])
    arrived(spread.at[pl.ds(0, NY - 1), :, 0], sent.at[11])
    arrived(spread.at[:, :, 0], sent.at[12])

    @pl.when(pivot_plane)
    def _():
        arrived(mbuf.at[:, pl.ds(0, (NY - 1) * KC)], sent.at[4])
        arrived(mrecv, sent.at[7])
        arrived(spread.at[0, pl.ds(0, NZ - 1), 0], sent.at[9])

    @pl.when(jnp.logical_and(gr == 0, gc < 4))
    def _():
        arrived(panel.at[pl.ds(0, 88), :], sent.at[6])

    @pl.when(jnp.logical_and(gr == 0, gc == 4))
    def _():
        arrived(panel.at[pl.ds(0, 96), :], sent.at[6])


def body(window, upper, panel, first):
    vmem, dma = pltpu.VMEM, pltpu.SemaphoreType.DMA
    spec = pl.BlockSpec(memory_space=pltpu.VMEM)

    return pl.pallas_call(
        kernel,
        out_shape=jax.ShapeDtypeStruct((ROWS, PW), F32),
        in_specs=[pl.BlockSpec(memory_space=pltpu.HBM)] * 4,
        out_specs=spec,
        scratch_shapes=[
            pltpu.SMEM((2,), jnp.int32),
            vmem((PW, NY * KC), BF16),
            vmem((8, NY * KC), jnp.int32),
            vmem((ROWS, PW), F32),
            vmem((NZ, ROWS, NY * KC), BF16),
            vmem((BLK, NY * KC), BF16),
            vmem((BLK, PW), F32),
            vmem((NZ - 1, 16, PW), F32),
            vmem((2, 8, PW), F32),
            vmem((2, 8, PW), F32),
            vmem((NY, NZ, NC, 8, PW), F32),
            vmem((7, ROWS, PW), F32),
            vmem((32, PARTS[0], PW), jnp.int16),
            vmem((32, 1, PW), F32),
            dma((3,)), dma((14,)),
            dma((NY - 1,)), dma, dma((NX - 1,)), dma, dma((NZ,)), dma, dma, dma, dma,
            dma((NZ - 1,)), dma((NY - 1,)), dma, dma((2, 4, 2)),
        ],
        compiler_params=pltpu.CompilerParams(
            collective_id=0, has_side_effects=True, vmem_limit_bytes=40 * 1024 * 1024
        ),
        name="panel_update",
    )(*[pltpu.with_memory_space_constraint(v, pltpu.HBM) for v in (window, upper.T, panel, first)])


def solution(mesh):
    return jax.shard_map(
        body,
        mesh=mesh,
        in_specs=(P("gr", "gc"), P("gc", "gr"), P(("gr", "gc"), None), P("gc")),
        out_specs=P(("gr", "gc"), None),
        check_vma=False,
    )
```

```python
import jax
import jax.numpy as jnp
from jax import lax
from jax.experimental import pallas as pl
from jax.experimental.pallas import tpu as pltpu
from jax.sharding import PartitionSpec as P

BLK = 128
NX, NC, NY, NZ = 4, 2, 4, 8
PW = 512
ROWS = 104
KC = 256
GW = 64
PARTS = (56, 48)
LEVELS = 32767.0
POWERS = 7
MESH = pl.DeviceIdType.MESH
F32 = jnp.float32
BF16 = jnp.bfloat16


def split(v):
    hi = v.astype(BF16)
    return hi, (v - hi.astype(F32)).astype(BF16)


def coded(v):
    step = jnp.maximum(jnp.max(jnp.abs(v), axis=0, keepdims=True) * (1.0 / LEVELS), 1e-37)
    return jnp.round(v * (1.0 / step)).astype(jnp.int32).astype(jnp.int16), step


def times_transposed(a, bt):
    return lax.dot_general(a, bt, (((1,), (1,)), ((), ())), preferred_element_type=F32)


def kernel(
    window, upper, panel, first_block, out,
    first, ut, thr, pown, abuf, mbuf, msend, mcodes, msteps, ppan, piece, spread,
    sums, codes, steps,
    loc, sent, uy_r, th_r, ux_r, uc_r, a_r, m_r, pan_r, mz_r, mzs_r, xs_r, zs_r, ys_r, cs_r, ring_r,
):
    gr, gc = lax.axis_index("gr"), lax.axis_index("gc")
    x, c = gr // NC, gr % NC
    z, y = gc // NY, gc % NY
    pivot_plane = gr == 0
    panel_source = jnp.logical_and(gr == 0, gc < 5)

    def at_y(d):
        return (gr, z * NY + (y + d) % NY)

    def at_z(d):
        return (gr, ((z + d) % NZ) * NY + y)

    def at_x(d):
        return (((x + d) % NX) * NC + c, gc)

    other_core = (x * NC + 1 - c, gc)

    def at_gr(d):
        return ((gr + d) % (NX * NC), gc)

    def remote(src, dst, s, r, who):
        return pltpu.make_async_remote_copy(
            src_ref=src, dst_ref=dst, send_sem=s, recv_sem=r, device_id=who, device_id_type=MESH
        )

    def arrived(like, sem):
        pltpu.make_async_copy(like, like, sem).wait()

    first_own = pltpu.make_async_copy(first_block, first, loc.at[2])
    first_own.start()

    barrier = pltpu.get_barrier_semaphore()
    for d in range(1, NY):
        pl.semaphore_signal(barrier, inc=1, device_id=at_y(d), device_id_type=MESH)
    for d in range(1, NX * NC):
        pl.semaphore_signal(barrier, inc=1, device_id=at_gr(d), device_id_type=MESH)
    for d in range(1, NZ):
        pl.semaphore_signal(barrier, inc=1, device_id=at_z(d), device_id_type=MESH)
    for s in range(2):
        owner = (16 * y + 2 * z + s) // 13

        @pl.when(jnp.logical_and(pivot_plane, owner != gc))
        def _():
            pl.semaphore_signal(barrier, inc=1, device_id=(0, owner), device_id_type=MESH)

    pl.semaphore_wait(barrier, 17 + jnp.where(panel_source, 11 + gc // 4, 0))

    def group(d):
        return pl.ds((((x + d) % NX) * NC + c) * GW, GW)

    def cols(d):
        return pl.ds(((y + d) % NY) * KC, KC)

    lane = lax.broadcasted_iota(jnp.int32, (8, KC), 1)
    first_own.wait()
    thr[:, pl.ds(y * KC, KC)] = jnp.where(lane < BLK, first[0], first[1]) * BLK
    uy = [remote(upper, ut.at[group(0), cols(0)], sent.at[0], uy_r.at[d - 1], at_y(d)) for d in range(1, NY)]
    th = [
        remote(thr.at[:, cols(0)], thr.at[:, cols(0)], sent.at[1], th_r, at_y(d)) for d in range(1, NY)
    ]
    ux = [
        [
            remote(ut.at[group(0), cols(-j)] if j else upper, ut.at[group(0), cols(-j)],
                   sent.at[2], ux_r.at[d - 1], at_x(d))
            for j in range(NY)
        ]
        for d in range(1, NX)
    ]
    upper_own = pltpu.make_async_copy(upper, ut.at[group(0), cols(0)], loc.at[0])
    panel_own = pltpu.make_async_copy(panel, pown, loc.at[1])
    for d in (1, 3, 2):
        uy[d - 1].start()
    for d in (1, 3, 2):
        ux[d - 1][0].start()
    for copy in th:
        copy.start()
    upper_own.start()

    mini = [
        remote(window.at[pl.ds(((y + d) % NY) * BLK, BLK), :], mbuf.at[:, pl.ds(y * KC, KC)],
               sent.at[4], m_r, at_y(d))
        for d in range(1, NY)
    ]
    mini_own = pltpu.make_async_copy(window.at[pl.ds(y * BLK, BLK), :], mbuf.at[:, pl.ds(y * KC, KC)], m_r)

    @pl.when(pivot_plane)
    def _():
        for copy in mini:
            copy.start()
        mini_own.start()

    order = (4, 3, 5, 2, 6, 1, 7, 0)

    def rows_of(i, yy):
        return pl.ds(pl.multiple_of((((z + order[i]) % NZ) * NY + yy) * ROWS, 8), ROWS)

    exchange, own_rows = [], []
    for i in range(NZ):
        exchange.append([
            remote(window.at[rows_of(i, (y + d) % NY), :], abuf.at[i, :, pl.ds(y * KC, KC)],
                   sent.at[5], a_r.at[i], at_y(d))
            for d in range(1, NY)
        ])
        own_rows.append(
            pltpu.make_async_copy(window.at[rows_of(i, y), :], abuf.at[i, :, pl.ds(y * KC, KC)], a_r.at[i])
        )
        for copy in exchange[i]:
            copy.start()
        own_rows[i].start()

    panel_own.start()

    def panel_piece(i):
        p = 13 * gc + i
        to = ((p % 16) // 2) * NY + p // 16
        return p, to

    for i in range(13):
        p, to = panel_piece(i)

        @pl.when(jnp.logical_and(jnp.logical_and(panel_source, p < 64), to != gc))
        def _():
            remote(panel.at[pl.ds(8 * i, 8), :], ppan.at[p % 2], sent.at[6], pan_r, (0, to)).start()

        @pl.when(jnp.logical_and(jnp.logical_and(panel_source, p < 64), to == gc))
        def _():
            pltpu.make_async_copy(panel.at[pl.ds(8 * i, 8), :], ppan.at[p % 2], pan_r).start()

    for j in (1, 3, 2):
        uy[j - 1].wait_recv()
        for d in (1, 3, 2):
            ux[d - 1][j].start()
    uc = [remote(ut.at[group(-d), :], ut.at[group(-d), :], sent.at[3], uc_r, other_core) for d in range(NX)]
    upper_own.wait()
    uc[0].start()
    for d in (1, 3, 2):
        arrived(ut.at[group(-d), :], ux_r.at[d - 1])
        uc[d].start()
    arrived(thr.at[:, pl.ds(0, (NY - 1) * KC)], th_r)
    arrived(ut.at[pl.ds(0, PW // NC), :], uc_r)

    def product(a, row0):
        ids = row0 + lax.broadcasted_iota(jnp.int32, a.shape, 0)
        kept = jnp.where(ids >= thr[0:1, :], a.astype(F32), 0.0).astype(BF16)
        return times_transposed(kept, ut[...])

    mz = [
        [
            remote(mcodes.at[(z + d) % NZ], mcodes.at[NZ + d - 1], sent.at[7], mz_r, at_z(d)),
            remote(msteps.at[(z + d) % NZ], msteps.at[NZ + d - 1], sent.at[14], mzs_r, at_z(d)),
        ]
        for d in range(1, NZ)
    ]

    @pl.when(pivot_plane)
    def _():
        arrived(mbuf, m_r)
        msend[...] = product(mbuf[...], y * BLK)
        for k in range(NZ):
            mcodes[k], msteps[k] = coded(msend[pl.ds(16 * k, 16), :])
        for d in (4, 3, 5, 2, 6, 1, 7):
            for copy in mz[d - 1]:
                copy.start()

    def chunk(i):
        arrived(abuf.at[i], a_r.at[i])
        return product(abuf[i], gr * (ROWS * NY * NZ) + (((z + order[i]) % NZ) * NY + y) * ROWS)

    parts = (pl.ds(0, PARTS[0]), pl.ds(PARTS[0], PARTS[1]))
    PLUS, MINUS = 0, 1
    hops = (at_z(1), at_z(NZ - 1))

    def message(way, k, h):
        at = 16 * way + 2 * k + h
        rows = pl.ds(0, PARTS[h])
        return [
            remote(codes.at[at, rows, :], codes.at[at + 8, rows, :], sent.at[8], ring_r.at[way, k, h], hops[way]),
            remote(steps.at[at], steps.at[at + 8], sent.at[13], ring_r.at[way, k, h], hops[way]),
        ]

    def send_on(way, k, h, v):
        at = 16 * way + 2 * k + h
        codes[at, pl.ds(0, PARTS[h]), :], steps[at] = coded(v)
        for copy in message(way, k, h):
            copy.start()

    def came(way, k, h):
        at = 16 * way + 2 * k + h + 8
        arrived(steps.at[pl.ds(0, PARTS[h] // 2 + 1)], ring_r.at[way, k, h])
        return codes[at, pl.ds(0, PARTS[h]), :].astype(jnp.int32).astype(F32) * steps[at]

    def forward(k, h):
        send_on(PLUS, k, h, sums[2 * k - 1, parts[h], :] + came(PLUS, k - 1, h))
        send_on(MINUS, k, 1 - h, sums[2 * k, parts[1 - h], :] + came(MINUS, k - 1, 1 - h))

    update = chunk(0)
    send_on(PLUS, 0, 0, update[: PARTS[0]])
    send_on(MINUS, 0, 1, update[PARTS[0] :])
    spread_x = [
        remote(piece.at[(d % NC)], spread.at[y, z, d % NC], sent.at[9], xs_r, (d, gc))
        for d in range(1, NX * NC)
    ]

    spread_z = [
        remote(spread.at[y, z, c], spread.at[y, z, c], sent.at[10], zs_r.at[d - 1], at_z(d)) for d in range(1, NZ)
    ]
    spread_y = [
        [
            remote(spread.at[y, (z + NZ - j) % NZ, c], spread.at[y, (z + NZ - j) % NZ, c],
                   sent.at[11], ys_r.at[d - 1], at_y(d))
            for j in range(NZ)
        ]
        for d in range(1, NY)
    ]

    def spread_own():
        for d in (1, 7, 2, 6, 3, 5, 4):
            spread_z[d - 1].start()
        for d in (1, 3, 2):
            spread_y[d - 1][0].start()

    @pl.when(pivot_plane)
    def _():
        arrived(mcodes.at[pl.ds(0, NZ - 1)], mz_r)
        arrived(msteps.at[pl.ds(0, NZ - 1)], mzs_r)
        arrived(ppan, pan_r)
        total = msend[pl.ds(z * 16, 16), :]
        for d in range(1, NZ):
            total = total + mcodes[NZ + d - 1].astype(jnp.int32).astype(F32) * msteps[NZ + d - 1]
        for s in range(2):
            piece[s] = ppan[s] - total[8 * s : 8 * s + 8]
        spread[y, z, 0] = piece[0]
        for d in (4, 5, 2, 3, 6, 7, 1):
            spread_x[d - 1].start()
        spread_own()

    sums[1] = chunk(1)
    send_on(PLUS, 1, 1, sums[1, parts[1], :])
    sums[2] = chunk(2)
    send_on(MINUS, 1, 0, sums[2, parts[0], :])
    forward(1, 0)
    sums[3] = chunk(3)
    sums[4] = chunk(4)
    forward(2, 1)

    forward(2, 0)

    @pl.when(jnp.logical_not(pivot_plane))
    def _():
        remote(piece.at[0], spread.at[y, z, c], sent.at[9], xs_r, (0, gc)).wait_recv()
        spread_own()


    def came_along_z(which):
        for j in which:
            spread_z[j - 1].wait_recv()
            for d in (1, 3, 2):
                spread_y[d - 1][j].start()

    came_along_z((1, 7))
    sums[5] = chunk(5)
    came_along_z((2, 6))
    sums[6] = chunk(6)
    forward(3, 1)
    forward(3, 0)

    came_along_z((3, 5, 4))
    spread_c = [
        remote(spread.at[(y + NY - d) % NY, :, c], spread.at[(y + NY - d) % NY, :, c], sent.at[12], cs_r, other_core)
        for d in range(NY)
    ]
    spread_c[0].start()

    sums[0] = chunk(7)
    panel_own.wait()
    for h in (1, 0):
        sums[0, parts[h], :] += came(PLUS, 3, h)
        sums[0, parts[1 - h], :] += came(MINUS, 3, 1 - h)
    schur = pown[...] - sums[0]

    for d in (1, 3, 2):
        arrived(spread.at[0, :, 0], ys_r.at[d - 1])
        spread_c[d].start()
    arrived(spread.at[:, :, 0], cs_r)

    pivot = spread[...].reshape(PW, PW)
    same = lax.broadcasted_iota(jnp.int32, (PW, PW), 0) == lax.broadcasted_iota(jnp.int32, (PW, PW), 1)
    scale = jnp.sum(jnp.sum(jnp.where(same, pivot, 0.0), axis=0, keepdims=True), axis=1, keepdims=True) / PW
    rest_hi, rest_lo = split(jnp.where(same, 1.0, 0.0) - pivot / scale)
    row_ids = (gr * NY * NZ + gc) * ROWS + lax.broadcasted_iota(jnp.int32, (ROWS, PW), 0)
    unit = jnp.where(row_ids == lax.broadcasted_iota(jnp.int32, (ROWS, PW), 1), 1.0, 0.0)
    left = jnp.where(row_ids < PW, unit, schur / scale)
    total = left
    for _ in range(POWERS):
        hi, lo = split(total)
        both = jnp.dot(jnp.concatenate([hi, lo]), rest_hi, preferred_element_type=F32)
        total = left + (both[:ROWS] + (both[ROWS:] + jnp.dot(hi, rest_lo, preferred_element_type=F32)))
    out[...] = total

    arrived(ut.at[pl.ds(0, 48), :], sent.at[0])
    arrived(thr.at[:, pl.ds(0, (NY - 1) * KC)], sent.at[1])
    arrived(ut.at[pl.ds(0, 3 * GW), :], sent.at[2])
    arrived(ut.at[pl.ds(0, PW // NC), :], sent.at[3])
    arrived(abuf.at[:, :, pl.ds(0, (NY - 1) * KC)], sent.at[5])
    arrived(codes.at[pl.ds(0, 13)], sent.at[8])
    arrived(steps.at[pl.ds(0, 14)], sent.at[13])
    arrived(spread.at[0, pl.ds(0, NZ - 1), 0], sent.at[10])
    arrived(spread.at[pl.ds(0, NY - 1), :, 0], sent.at[11])
    arrived(spread.at[:, :, 0], sent.at[12])

    @pl.when(pivot_plane)
    def _():
        arrived(mbuf.at[:, pl.ds(0, (NY - 1) * KC)], sent.at[4])
        arrived(mcodes.at[pl.ds(0, NZ - 1)], sent.at[7])
        arrived(msteps.at[pl.ds(0, NZ - 1)], sent.at[14])
        arrived(spread.at[0, pl.ds(0, NZ - 1), 0], sent.at[9])

    @pl.when(jnp.logical_and(gr == 0, gc < 4))
    def _():
        arrived(panel.at[pl.ds(0, 88), :], sent.at[6])

    @pl.when(jnp.logical_and(gr == 0, gc == 4))
    def _():
        arrived(panel.at[pl.ds(0, 96), :], sent.at[6])


def body(window, upper, panel, first):
    vmem, dma = pltpu.VMEM, pltpu.SemaphoreType.DMA
    spec = pl.BlockSpec(memory_space=pltpu.VMEM)

    return pl.pallas_call(
        kernel,
        out_shape=jax.ShapeDtypeStruct((ROWS, PW), F32),
        in_specs=[pl.BlockSpec(memory_space=pltpu.HBM)] * 4,
        out_specs=spec,
        scratch_shapes=[
            pltpu.SMEM((2,), jnp.int32),
            vmem((PW, NY * KC), BF16),
            vmem((8, NY * KC), jnp.int32),
            vmem((ROWS, PW), F32),
            vmem((NZ, ROWS, NY * KC), BF16),
            vmem((BLK, NY * KC), BF16),
            vmem((BLK, PW), F32),
            vmem((2 * NZ - 1, 16, PW), jnp.int16),
            vmem((2 * NZ - 1, 1, PW), F32),
            vmem((2, 8, PW), F32),
            vmem((2, 8, PW), F32),
            vmem((NY, NZ, NC, 8, PW), F32),
            vmem((7, ROWS, PW), F32),
            vmem((32, PARTS[0], PW), jnp.int16),
            vmem((32, 1, PW), F32),
            dma((3,)), dma((15,)),
            dma((NY - 1,)), dma, dma((NX - 1,)), dma, dma((NZ,)), dma, dma, dma, dma, dma,
            dma((NZ - 1,)), dma((NY - 1,)), dma, dma((2, 4, 2)),
        ],
        compiler_params=pltpu.CompilerParams(
            collective_id=0, has_side_effects=True, vmem_limit_bytes=40 * 1024 * 1024
        ),
        name="panel_update",
    )(*[pltpu.with_memory_space_constraint(v, pltpu.HBM) for v in (window, upper.T, panel, first)])


def solution(mesh):
    return jax.shard_map(
        body,
        mesh=mesh,
        in_specs=(P("gr", "gc"), P("gc", "gr"), P(("gr", "gc"), None), P("gc")),
        out_specs=P(("gr", "gc"), None),
        check_vma=False,
    )
```

```python
import jax
import jax.numpy as jnp
from jax import lax
from jax.experimental import pallas as pl
from jax.experimental.pallas import tpu as pltpu
from jax.sharding import PartitionSpec as P

BLK = 128
NX, NC, NY, NZ = 4, 2, 4, 8
PW = 512
ROWS = 104
KC = 256
GW = 64
PARTS = (56, 48)
LEVELS = 32767.0
POWERS = 7
MESH = pl.DeviceIdType.MESH
F32 = jnp.float32
BF16 = jnp.bfloat16


def split(v):
    hi = v.astype(BF16)
    return hi, (v - hi.astype(F32)).astype(BF16)


def coded(v):
    step = jnp.maximum(jnp.max(jnp.abs(v), axis=0, keepdims=True) * (1.0 / LEVELS), 1e-37)
    return jnp.round(v * (1.0 / step)).astype(jnp.int32).astype(jnp.int16), step


def times_transposed(a, bt):
    return lax.dot_general(a, bt, (((1,), (1,)), ((), ())), preferred_element_type=F32)


def kernel(
    window, upper, panel, first_block, out,
    first, ut, thr, pown, abuf, mbuf, msend, mcodes, msteps, ppan, piece, spread,
    sums, codes, steps,
    loc, sent, uy_r, th_r, ux_r, uc_r, a_r, m_r, pan_r, mz_r, mzs_r, xs_r, zs_r, ys_r, cs_r, ring_r,
):
    gr, gc = lax.axis_index("gr"), lax.axis_index("gc")
    x, c = gr // NC, gr % NC
    z, y = gc // NY, gc % NY
    pivot_plane = gr == 0
    panel_source = jnp.logical_and(gr == 0, gc < 5)

    def at_y(d):
        return (gr, z * NY + (y + d) % NY)

    def at_z(d):
        return (gr, ((z + d) % NZ) * NY + y)

    def at_x(d):
        return (((x + d) % NX) * NC + c, gc)

    other_core = (x * NC + 1 - c, gc)

    def at_gr(d):
        return ((gr + d) % (NX * NC), gc)

    def remote(src, dst, s, r, who):
        return pltpu.make_async_remote_copy(
            src_ref=src, dst_ref=dst, send_sem=s, recv_sem=r, device_id=who, device_id_type=MESH
        )

    def arrived(like, sem):
        pltpu.make_async_copy(like, like, sem).wait()

    first_own = pltpu.make_async_copy(first_block, first, loc.at[2])
    first_own.start()

    barrier = pltpu.get_barrier_semaphore()
    for d in range(1, NY):
        pl.semaphore_signal(barrier, inc=1, device_id=at_y(d), device_id_type=MESH)
    for d in range(1, NX * NC):
        pl.semaphore_signal(barrier, inc=1, device_id=at_gr(d), device_id_type=MESH)
    for d in range(1, NZ):
        pl.semaphore_signal(barrier, inc=1, device_id=at_z(d), device_id_type=MESH)
    for s in range(2):
        owner = (16 * y + 2 * z + s) // 13

        @pl.when(jnp.logical_and(pivot_plane, owner != gc))
        def _():
            pl.semaphore_signal(barrier, inc=1, device_id=(0, owner), device_id_type=MESH)

    pl.semaphore_wait(barrier, 17 + jnp.where(panel_source, 11 + gc // 4, 0))

    def group(d):
        return pl.ds((((x + d) % NX) * NC + c) * GW, GW)

    def cols(d):
        return pl.ds(((y + d) % NY) * KC, KC)

    lane = lax.broadcasted_iota(jnp.int32, (8, KC), 1)
    first_own.wait()
    thr[:, pl.ds(y * KC, KC)] = jnp.where(lane < BLK, first[0], first[1]) * BLK
    uy = [remote(upper, ut.at[group(0), cols(0)], sent.at[0], uy_r.at[d - 1], at_y(d)) for d in range(1, NY)]
    th = [
        remote(thr.at[:, cols(0)], thr.at[:, cols(0)], sent.at[1], th_r, at_y(d)) for d in range(1, NY)
    ]
    ux = [
        [
            remote(ut.at[group(0), cols(-j)] if j else upper, ut.at[group(0), cols(-j)],
                   sent.at[2], ux_r.at[d - 1], at_x(d))
            for j in range(NY)
        ]
        for d in range(1, NX)
    ]
    upper_own = pltpu.make_async_copy(upper, ut.at[group(0), cols(0)], loc.at[0])
    panel_own = pltpu.make_async_copy(panel, pown, loc.at[1])
    for d in (1, 3, 2):
        uy[d - 1].start()
    for d in (1, 3, 2):
        ux[d - 1][0].start()
    for copy in th:
        copy.start()
    upper_own.start()

    mini = [
        remote(window.at[pl.ds(((y + d) % NY) * BLK, BLK), :], mbuf.at[:, pl.ds(y * KC, KC)],
               sent.at[4], m_r, at_y(d))
        for d in range(1, NY)
    ]
    mini_own = pltpu.make_async_copy(window.at[pl.ds(y * BLK, BLK), :], mbuf.at[:, pl.ds(y * KC, KC)], m_r)

    @pl.when(pivot_plane)
    def _():
        for copy in mini:
            copy.start()
        mini_own.start()

    order = (4, 3, 5, 2, 6, 1, 7, 0)

    def rows_of(i, yy):
        return pl.ds(pl.multiple_of((((z + order[i]) % NZ) * NY + yy) * ROWS, 8), ROWS)

    exchange, own_rows = [], []
    for i in range(NZ):
        exchange.append([
            remote(window.at[rows_of(i, (y + d) % NY), :], abuf.at[i, :, pl.ds(y * KC, KC)],
                   sent.at[5], a_r.at[i], at_y(d))
            for d in range(1, NY)
        ])
        own_rows.append(
            pltpu.make_async_copy(window.at[rows_of(i, y), :], abuf.at[i, :, pl.ds(y * KC, KC)], a_r.at[i])
        )
        for copy in exchange[i]:
            copy.start()
        own_rows[i].start()

    panel_own.start()

    def panel_piece(i):
        p = 13 * gc + i
        to = ((p % 16) // 2) * NY + p // 16
        return p, to

    for i in range(13):
        p, to = panel_piece(i)

        @pl.when(jnp.logical_and(jnp.logical_and(panel_source, p < 64), to != gc))
        def _():
            remote(panel.at[pl.ds(8 * i, 8), :], ppan.at[p % 2], sent.at[6], pan_r, (0, to)).start()

        @pl.when(jnp.logical_and(jnp.logical_and(panel_source, p < 64), to == gc))
        def _():
            pltpu.make_async_copy(panel.at[pl.ds(8 * i, 8), :], ppan.at[p % 2], pan_r).start()

    for j in (1, 3, 2):
        uy[j - 1].wait_recv()
        for d in (1, 3, 2):
            ux[d - 1][j].start()
    uc = [remote(ut.at[group(-d), :], ut.at[group(-d), :], sent.at[3], uc_r, other_core) for d in range(NX)]
    upper_own.wait()
    uc[0].start()
    for d in (1, 3, 2):
        arrived(ut.at[group(-d), :], ux_r.at[d - 1])
        uc[d].start()
    arrived(thr.at[:, pl.ds(0, (NY - 1) * KC)], th_r)
    arrived(ut.at[pl.ds(0, PW // NC), :], uc_r)

    def product(a, row0):
        ids = row0 + lax.broadcasted_iota(jnp.int32, a.shape, 0)
        kept = jnp.where(ids >= thr[0:1, :], a.astype(F32), 0.0).astype(BF16)
        return times_transposed(kept, ut[...])

    mz = [
        [
            remote(mcodes.at[(z + d) % NZ], mcodes.at[NZ + d - 1], sent.at[7], mz_r, at_z(d)),
            remote(msteps.at[(z + d) % NZ], msteps.at[NZ + d - 1], sent.at[14], mzs_r, at_z(d)),
        ]
        for d in range(1, NZ)
    ]

    @pl.when(pivot_plane)
    def _():
        arrived(mbuf, m_r)
        msend[...] = product(mbuf[...], y * BLK)
        for k in range(NZ):
            mcodes[k], msteps[k] = coded(msend[pl.ds(16 * k, 16), :])
        for d in (4, 3, 5, 2, 6, 1, 7):
            for copy in mz[d - 1]:
                copy.start()

    def chunk(i):
        arrived(abuf.at[i], a_r.at[i])
        return product(abuf[i], gr * (ROWS * NY * NZ) + (((z + order[i]) % NZ) * NY + y) * ROWS)

    parts = (pl.ds(0, PARTS[0]), pl.ds(PARTS[0], PARTS[1]))
    PLUS, MINUS = 0, 1
    hops = (at_z(1), at_z(NZ - 1))

    def message(way, k, h):
        at = 16 * way + 2 * k + h
        rows = pl.ds(0, PARTS[h])
        return [
            remote(codes.at[at, rows, :], codes.at[at + 8, rows, :], sent.at[8], ring_r.at[way, k, h], hops[way]),
            remote(steps.at[at], steps.at[at + 8], sent.at[13], ring_r.at[way, k, h], hops[way]),
        ]

    def send_on(way, k, h, v):
        at = 16 * way + 2 * k + h
        codes[at, pl.ds(0, PARTS[h]), :], steps[at] = coded(v)
        for copy in message(way, k, h):
            copy.start()

    def came(way, k, h):
        at = 16 * way + 2 * k + h + 8
        arrived(steps.at[pl.ds(0, PARTS[h] // 2 + 1)], ring_r.at[way, k, h])
        return codes[at, pl.ds(0, PARTS[h]), :].astype(jnp.int32).astype(F32) * steps[at]

    def forward(k, h):
        send_on(PLUS, k, h, sums[2 * k - 1, parts[h], :] + came(PLUS, k - 1, h))
        send_on(MINUS, k, 1 - h, sums[2 * k, parts[1 - h], :] + came(MINUS, k - 1, 1 - h))

    update = chunk(0)
    send_on(PLUS, 0, 0, update[: PARTS[0]])
    send_on(MINUS, 0, 1, update[PARTS[0] :])
    spread_x = [
        remote(piece.at[(d % NC)], spread.at[y, z, d % NC], sent.at[9], xs_r, (d, gc))
        for d in range(1, NX * NC)
    ]

    spread_z = [
        remote(spread.at[y, z, c], spread.at[y, z, c], sent.at[10], zs_r.at[d - 1], at_z(d)) for d in range(1, NZ)
    ]
    spread_y = [
        [
            remote(spread.at[y, (z + NZ - j) % NZ, c], spread.at[y, (z + NZ - j) % NZ, c],
                   sent.at[11], ys_r.at[d - 1], at_y(d))
            for j in range(NZ)
        ]
        for d in range(1, NY)
    ]

    def spread_own():
        for d in (1, 7, 2, 6, 3, 5, 4):
            spread_z[d - 1].start()
        for d in (1, 3, 2):
            spread_y[d - 1][0].start()

    @pl.when(pivot_plane)
    def _():
        arrived(mcodes.at[pl.ds(0, NZ - 1)], mz_r)
        arrived(msteps.at[pl.ds(0, NZ - 1)], mzs_r)
        arrived(ppan, pan_r)
        total = msend[pl.ds(z * 16, 16), :]
        for d in range(1, NZ):
            total = total + mcodes[NZ + d - 1].astype(jnp.int32).astype(F32) * msteps[NZ + d - 1]
        for s in range(2):
            piece[s] = ppan[s] - total[8 * s : 8 * s + 8]
        spread[y, z, 0] = piece[0]
        for d in (4, 5, 2, 3, 6, 7, 1):
            spread_x[d - 1].start()
        spread_own()

    sums[1] = chunk(1)
    send_on(PLUS, 1, 1, sums[1, parts[1], :])
    other_planes = jnp.logical_not(pivot_plane)

    def came_along_z(which, where):
        @pl.when(where)
        def _():
            for j in which:
                spread_z[j - 1].wait_recv()
                for d in (1, 3, 2):
                    spread_y[d - 1][j].start()

    sums[2] = chunk(2)
    send_on(MINUS, 1, 0, sums[2, parts[0], :])
    forward(1, 0)
    sums[3] = chunk(3)
    sums[4] = chunk(4)
    came_along_z((1, 7, 2, 6), pivot_plane)
    forward(2, 1)

    @pl.when(jnp.logical_not(pivot_plane))
    def _():
        remote(piece.at[0], spread.at[y, z, c], sent.at[9], xs_r, (0, gc)).wait_recv()
        spread_own()


    came_along_z((3, 5, 4), pivot_plane)
    forward(2, 0)

    came_along_z((1, 7), other_planes)
    sums[5] = chunk(5)
    came_along_z((2, 6), other_planes)
    sums[6] = chunk(6)
    forward(3, 1)
    forward(3, 0)

    came_along_z((3, 5, 4), other_planes)
    spread_c = [
        remote(spread.at[(y + NY - d) % NY, :, c], spread.at[(y + NY - d) % NY, :, c], sent.at[12], cs_r, other_core)
        for d in range(NY)
    ]
    spread_c[0].start()

    def came_along_y(where):
        @pl.when(where)
        def _():
            for d in (1, 3, 2):
                arrived(spread.at[0, :, 0], ys_r.at[d - 1])
                spread_c[d].start()

    came_along_y(gr >= 0)

    sums[0] = chunk(7)
    panel_own.wait()
    for h in (1, 0):
        sums[0, parts[h], :] += came(PLUS, 3, h)
        sums[0, parts[1 - h], :] += came(MINUS, 3, 1 - h)
    schur = pown[...] - sums[0]

    arrived(spread.at[:, :, 0], cs_r)

    pivot = spread[...].reshape(PW, PW)
    same = lax.broadcasted_iota(jnp.int32, (BLK, BLK), 0) == lax.broadcasted_iota(jnp.int32, (BLK, BLK), 1)
    diagonal = [jnp.where(same, pivot[k : k + BLK, k : k + BLK], 0.0) for k in range(0, PW, BLK)]
    diagonal = (diagonal[0] + diagonal[1]) + (diagonal[2] + diagonal[3])
    scale = jnp.sum(jnp.sum(diagonal, axis=0, keepdims=True), axis=1, keepdims=True) / PW
    near = jnp.where(jnp.abs(scale) > 1.0, 2.0**-64, 2.0**64)
    inverse_scale = 1.0 / (scale * near)
    same = lax.broadcasted_iota(jnp.int32, (PW, PW), 0) == lax.broadcasted_iota(jnp.int32, (PW, PW), 1)
    rest_hi, rest_lo = split(jnp.where(same, 1.0, 0.0) - (pivot * near) * inverse_scale)
    row_ids = (gr * NY * NZ + gc) * ROWS + lax.broadcasted_iota(jnp.int32, (ROWS, PW), 0)
    unit = jnp.where(row_ids == lax.broadcasted_iota(jnp.int32, (ROWS, PW), 1), 1.0, 0.0)
    left = jnp.where(row_ids < PW, unit, schur / scale)
    total = left
    for _ in range(POWERS):
        hi, lo = split(total)
        both = jnp.dot(jnp.concatenate([hi, lo]), rest_hi, preferred_element_type=F32)
        total = left + (both[:ROWS] + (both[ROWS:] + jnp.dot(hi, rest_lo, preferred_element_type=F32)))
    out[...] = total

    arrived(ut.at[pl.ds(0, 48), :], sent.at[0])
    arrived(thr.at[:, pl.ds(0, (NY - 1) * KC)], sent.at[1])
    arrived(ut.at[pl.ds(0, 3 * GW), :], sent.at[2])
    arrived(ut.at[pl.ds(0, PW // NC), :], sent.at[3])
    arrived(abuf.at[:, :, pl.ds(0, (NY - 1) * KC)], sent.at[5])
    arrived(codes.at[pl.ds(0, 13)], sent.at[8])
    arrived(steps.at[pl.ds(0, 14)], sent.at[13])
    arrived(spread.at[0, pl.ds(0, NZ - 1), 0], sent.at[10])
    arrived(spread.at[pl.ds(0, NY - 1), :, 0], sent.at[11])
    arrived(spread.at[:, :, 0], sent.at[12])

    @pl.when(pivot_plane)
    def _():
        arrived(mbuf.at[:, pl.ds(0, (NY - 1) * KC)], sent.at[4])
        arrived(mcodes.at[pl.ds(0, NZ - 1)], sent.at[7])
        arrived(msteps.at[pl.ds(0, NZ - 1)], sent.at[14])
        arrived(spread.at[0, pl.ds(0, NZ - 1), 0], sent.at[9])

    @pl.when(jnp.logical_and(gr == 0, gc < 4))
    def _():
        arrived(panel.at[pl.ds(0, 88), :], sent.at[6])

    @pl.when(jnp.logical_and(gr == 0, gc == 4))
    def _():
        arrived(panel.at[pl.ds(0, 96), :], sent.at[6])


def body(window, upper, panel, first):
    vmem, dma = pltpu.VMEM, pltpu.SemaphoreType.DMA
    spec = pl.BlockSpec(memory_space=pltpu.VMEM)

    return pl.pallas_call(
        kernel,
        out_shape=jax.ShapeDtypeStruct((ROWS, PW), F32),
        in_specs=[pl.BlockSpec(memory_space=pltpu.HBM)] * 4,
        out_specs=spec,
        scratch_shapes=[
            pltpu.SMEM((2,), jnp.int32),
            vmem((PW, NY * KC), BF16),
            vmem((8, NY * KC), jnp.int32),
            vmem((ROWS, PW), F32),
            vmem((NZ, ROWS, NY * KC), BF16),
            vmem((BLK, NY * KC), BF16),
            vmem((BLK, PW), F32),
            vmem((2 * NZ - 1, 16, PW), jnp.int16),
            vmem((2 * NZ - 1, 1, PW), F32),
            vmem((2, 8, PW), F32),
            vmem((2, 8, PW), F32),
            vmem((NY, NZ, NC, 8, PW), F32),
            vmem((7, ROWS, PW), F32),
            vmem((32, PARTS[0], PW), jnp.int16),
            vmem((32, 1, PW), F32),
            dma((3,)), dma((15,)),
            dma((NY - 1,)), dma, dma((NX - 1,)), dma, dma((NZ,)), dma, dma, dma, dma, dma,
            dma((NZ - 1,)), dma((NY - 1,)), dma, dma((2, 4, 2)),
        ],
        compiler_params=pltpu.CompilerParams(
            collective_id=0, has_side_effects=True, vmem_limit_bytes=40 * 1024 * 1024
        ),
        name="panel_update",
    )(*[pltpu.with_memory_space_constraint(v, pltpu.HBM) for v in (window, upper.T, panel, first)])


def solution(mesh):
    return jax.shard_map(
        body,
        mesh=mesh,
        in_specs=(P("gr", "gc"), P("gc", "gr"), P(("gr", "gc"), None), P("gc")),
        out_specs=P(("gr", "gc"), None),
        check_vma=False,
    )
```

```python
import jax
import jax.numpy as jnp
from jax import lax
from jax.experimental import pallas as pl
from jax.experimental.pallas import tpu as pltpu
from jax.sharding import PartitionSpec as P

BLK = 128
NX, NC, NY, NZ = 4, 2, 4, 8
PW = 512
ROWS = 104
KC = 256
GW = 64
PARTS = (56, 48)
LEVELS = 32767.0
POWERS = 7
MESH = pl.DeviceIdType.MESH
F32 = jnp.float32
BF16 = jnp.bfloat16


def split(v):
    hi = v.astype(BF16)
    return hi, (v - hi.astype(F32)).astype(BF16)


def coded(v):
    step = jnp.maximum(jnp.max(jnp.abs(v), axis=0, keepdims=True) * (1.0 / LEVELS), 1e-37)
    return jnp.round(v * (1.0 / step)).astype(jnp.int32).astype(jnp.int16), step


def times_transposed(a, bt):
    return lax.dot_general(a, bt, (((1,), (1,)), ((), ())), preferred_element_type=F32)


def kernel(
    window, upper, panel, first_block, out,
    first, ut, thr, pown, abuf, mbuf, msend, mcodes, msteps, ppan, piece, spread,
    sums, codes, steps,
    loc, sent, uy_r, th_r, ux_r, uc_r, a_r, m_r, pan_r, mz_r, mzs_r, xs_r, zs_r, ys_r, cs_r, ring_r,
):
    gr, gc = lax.axis_index("gr"), lax.axis_index("gc")
    x, c = gr // NC, gr % NC
    z, y = gc // NY, gc % NY
    pivot_plane = gr == 0
    panel_source = jnp.logical_and(gr == 0, gc < 5)

    def at_y(d):
        return (gr, z * NY + (y + d) % NY)

    def at_z(d):
        return (gr, ((z + d) % NZ) * NY + y)

    def at_x(d):
        return (((x + d) % NX) * NC + c, gc)

    other_core = (x * NC + 1 - c, gc)

    def at_gr(d):
        return ((gr + d) % (NX * NC), gc)

    def remote(src, dst, s, r, who):
        return pltpu.make_async_remote_copy(
            src_ref=src, dst_ref=dst, send_sem=s, recv_sem=r, device_id=who, device_id_type=MESH
        )

    def arrived(like, sem):
        pltpu.make_async_copy(like, like, sem).wait()

    first_own = pltpu.make_async_copy(first_block, first, loc.at[2])
    first_own.start()

    barrier = pltpu.get_barrier_semaphore()
    for d in range(1, NY):
        pl.semaphore_signal(barrier, inc=1, device_id=at_y(d), device_id_type=MESH)
    for d in range(1, NX * NC):
        pl.semaphore_signal(barrier, inc=1, device_id=at_gr(d), device_id_type=MESH)
    for d in range(1, NZ):
        pl.semaphore_signal(barrier, inc=1, device_id=at_z(d), device_id_type=MESH)
    for s in range(2):
        owner = (16 * y + 2 * z + s) // 13

        @pl.when(jnp.logical_and(pivot_plane, owner != gc))
        def _():
            pl.semaphore_signal(barrier, inc=1, device_id=(0, owner), device_id_type=MESH)

    def group(d):
        return pl.ds((((x + d) % NX) * NC + c) * GW, GW)

    def cols(d):
        return pl.ds(((y + d) % NY) * KC, KC)

    upper_own = pltpu.make_async_copy(upper, ut.at[group(0), cols(0)], loc.at[0])
    upper_own.start()
    lane = lax.broadcasted_iota(jnp.int32, (8, KC), 1)
    first_own.wait()
    thr[:, pl.ds(y * KC, KC)] = jnp.where(lane < BLK, first[0], first[1]) * BLK
    upper_own.wait()

    pl.semaphore_wait(barrier, 17 + jnp.where(panel_source, 11 + gc // 4, 0))

    uy = [remote(ut.at[group(0), cols(0)], ut.at[group(0), cols(0)], sent.at[0], uy_r.at[d - 1], at_y(d)) for d in range(1, NY)]
    th = [
        remote(thr.at[:, cols(0)], thr.at[:, cols(0)], sent.at[1], th_r, at_y(d)) for d in range(1, NY)
    ]
    ux = [
        [
            remote(ut.at[group(0), cols(-j)], ut.at[group(0), cols(-j)],
                   sent.at[2], ux_r.at[d - 1], at_x(d))
            for j in range(NY)
        ]
        for d in range(1, NX)
    ]
    panel_own = pltpu.make_async_copy(panel, pown, loc.at[1])
    for d in (1, 3, 2):
        uy[d - 1].start()
    for d in (1, 3, 2):
        ux[d - 1][0].start()
    for copy in th:
        copy.start()

    mini = [
        remote(window.at[pl.ds(((y + d) % NY) * BLK, BLK), :], mbuf.at[:, pl.ds(y * KC, KC)],
               sent.at[4], m_r, at_y(d))
        for d in range(1, NY)
    ]
    mini_own = pltpu.make_async_copy(window.at[pl.ds(y * BLK, BLK), :], mbuf.at[:, pl.ds(y * KC, KC)], m_r)

    @pl.when(pivot_plane)
    def _():
        for copy in mini:
            copy.start()
        mini_own.start()

    order = (4, 3, 5, 2, 6, 1, 7, 0)

    def rows_of(i, yy):
        return pl.ds(pl.multiple_of((((z + order[i]) % NZ) * NY + yy) * ROWS, 8), ROWS)

    exchange, own_rows = [], []
    for i in range(NZ):
        exchange.append([
            remote(window.at[rows_of(i, (y + d) % NY), :], abuf.at[i, :, pl.ds(y * KC, KC)],
                   sent.at[5], a_r.at[i], at_y(d))
            for d in range(1, NY)
        ])
        own_rows.append(
            pltpu.make_async_copy(window.at[rows_of(i, y), :], abuf.at[i, :, pl.ds(y * KC, KC)], a_r.at[i])
        )
        for copy in exchange[i]:
            copy.start()
        own_rows[i].start()

    panel_own.start()

    def panel_piece(i):
        p = 13 * gc + i
        to = ((p % 16) // 2) * NY + p // 16
        return p, to

    for i in range(13):
        p, to = panel_piece(i)

        @pl.when(jnp.logical_and(jnp.logical_and(panel_source, p < 64), to != gc))
        def _():
            remote(panel.at[pl.ds(8 * i, 8), :], ppan.at[p % 2], sent.at[6], pan_r, (0, to)).start()

        @pl.when(jnp.logical_and(jnp.logical_and(panel_source, p < 64), to == gc))
        def _():
            pltpu.make_async_copy(panel.at[pl.ds(8 * i, 8), :], ppan.at[p % 2], pan_r).start()

    for j in (1, 3, 2):
        uy[j - 1].wait_recv()
        for d in (1, 3, 2):
            ux[d - 1][j].start()
    uc = [remote(ut.at[group(-d), :], ut.at[group(-d), :], sent.at[3], uc_r, other_core) for d in range(NX)]
    uc[0].start()
    for d in (1, 3, 2):
        arrived(ut.at[group(-d), :], ux_r.at[d - 1])
        uc[d].start()
    arrived(thr.at[:, pl.ds(0, (NY - 1) * KC)], th_r)
    arrived(ut.at[pl.ds(0, PW // NC), :], uc_r)

    def product(a, row0):
        ids = row0 + lax.broadcasted_iota(jnp.int32, a.shape, 0)
        kept = jnp.where(ids >= thr[0:1, :], a.astype(F32), 0.0).astype(BF16)
        return times_transposed(kept, ut[...])

    mz = [
        [
            remote(mcodes.at[(z + d) % NZ], mcodes.at[NZ + d - 1], sent.at[7], mz_r, at_z(d)),
            remote(msteps.at[(z + d) % NZ], msteps.at[NZ + d - 1], sent.at[14], mzs_r, at_z(d)),
        ]
        for d in range(1, NZ)
    ]

    @pl.when(pivot_plane)
    def _():
        arrived(mbuf, m_r)
        msend[...] = product(mbuf[...], y * BLK)
        for k in range(NZ):
            mcodes[k], msteps[k] = coded(msend[pl.ds(16 * k, 16), :])
        for d in (4, 3, 5, 2, 6, 1, 7):
            for copy in mz[d - 1]:
                copy.start()

    def chunk(i):
        arrived(abuf.at[i], a_r.at[i])
        return product(abuf[i], gr * (ROWS * NY * NZ) + (((z + order[i]) % NZ) * NY + y) * ROWS)

    parts = (pl.ds(0, PARTS[0]), pl.ds(PARTS[0], PARTS[1]))
    PLUS, MINUS = 0, 1
    hops = (at_z(1), at_z(NZ - 1))

    def message(way, k, h):
        at = 16 * way + 2 * k + h
        rows = pl.ds(0, PARTS[h])
        return [
            remote(codes.at[at, rows, :], codes.at[at + 8, rows, :], sent.at[8], ring_r.at[way, k, h], hops[way]),
            remote(steps.at[at], steps.at[at + 8], sent.at[13], ring_r.at[way, k, h], hops[way]),
        ]

    def send_on(way, k, h, v):
        at = 16 * way + 2 * k + h
        codes[at, pl.ds(0, PARTS[h]), :], steps[at] = coded(v)
        for copy in message(way, k, h):
            copy.start()

    def came(way, k, h):
        at = 16 * way + 2 * k + h + 8
        arrived(steps.at[pl.ds(0, PARTS[h] // 2 + 1)], ring_r.at[way, k, h])
        return codes[at, pl.ds(0, PARTS[h]), :].astype(jnp.int32).astype(F32) * steps[at]

    def forward(k, h):
        send_on(PLUS, k, h, sums[2 * k - 1, parts[h], :] + came(PLUS, k - 1, h))
        send_on(MINUS, k, 1 - h, sums[2 * k, parts[1 - h], :] + came(MINUS, k - 1, 1 - h))

    update = chunk(0)
    send_on(PLUS, 0, 0, update[: PARTS[0]])
    send_on(MINUS, 0, 1, update[PARTS[0] :])
    spread_x = [
        remote(piece.at[(d % NC)], spread.at[y, z, d % NC], sent.at[9], xs_r, (d, gc))
        for d in range(1, NX * NC)
    ]

    spread_z = [
        remote(spread.at[y, z, c], spread.at[y, z, c], sent.at[10], zs_r.at[d - 1], at_z(d)) for d in range(1, NZ)
    ]
    spread_y = [
        [
            remote(spread.at[y, (z + NZ - j) % NZ, c], spread.at[y, (z + NZ - j) % NZ, c],
                   sent.at[11], ys_r.at[d - 1], at_y(d))
            for j in range(NZ)
        ]
        for d in range(1, NY)
    ]

    def spread_own():
        for d in (1, 7, 2, 6, 3, 5, 4):
            spread_z[d - 1].start()
        for d in (1, 3, 2):
            spread_y[d - 1][0].start()

    @pl.when(pivot_plane)
    def _():
        arrived(mcodes.at[pl.ds(0, NZ - 1)], mz_r)
        arrived(msteps.at[pl.ds(0, NZ - 1)], mzs_r)
        arrived(ppan, pan_r)
        total = msend[pl.ds(z * 16, 16), :]
        for d in range(1, NZ):
            total = total + mcodes[NZ + d - 1].astype(jnp.int32).astype(F32) * msteps[NZ + d - 1]
        for s in range(2):
            piece[s] = ppan[s] - total[8 * s : 8 * s + 8]
        spread[y, z, 0] = piece[0]
        for d in (4, 5, 2, 3, 6, 7, 1):
            spread_x[d - 1].start()
        spread_own()

    sums[1] = chunk(1)
    send_on(PLUS, 1, 1, sums[1, parts[1], :])
    other_planes = jnp.logical_not(pivot_plane)

    def came_along_z(which, where):
        @pl.when(where)
        def _():
            for j in which:
                spread_z[j - 1].wait_recv()
                for d in (1, 3, 2):
                    spread_y[d - 1][j].start()

    sums[2] = chunk(2)
    send_on(MINUS, 1, 0, sums[2, parts[0], :])
    forward(1, 0)
    sums[3] = chunk(3)
    sums[4] = chunk(4)
    came_along_z((1, 7, 2, 6), pivot_plane)
    forward(2, 1)

    @pl.when(jnp.logical_not(pivot_plane))
    def _():
        remote(piece.at[0], spread.at[y, z, c], sent.at[9], xs_r, (0, gc)).wait_recv()
        spread_own()


    came_along_z((3, 5, 4), pivot_plane)
    forward(2, 0)

    came_along_z((1, 7), other_planes)
    sums[5] = chunk(5)
    came_along_z((2, 6), other_planes)
    sums[6] = chunk(6)
    forward(3, 1)
    forward(3, 0)

    came_along_z((3, 5, 4), other_planes)
    spread_c = [
        remote(spread.at[(y + NY - d) % NY, :, c], spread.at[(y + NY - d) % NY, :, c], sent.at[12], cs_r, other_core)
        for d in range(NY)
    ]
    spread_c[0].start()

    def came_along_y(where):
        @pl.when(where)
        def _():
            for d in (1, 3, 2):
                arrived(spread.at[0, :, 0], ys_r.at[d - 1])
                spread_c[d].start()

    came_along_y(gr >= 0)

    sums[0] = chunk(7)
    panel_own.wait()
    for h in (1, 0):
        sums[0, parts[h], :] += came(PLUS, 3, h)
        sums[0, parts[1 - h], :] += came(MINUS, 3, 1 - h)
    schur = pown[...] - sums[0]

    arrived(spread.at[:, :, 0], cs_r)

    pivot = spread[...].reshape(PW, PW)
    same = lax.broadcasted_iota(jnp.int32, (BLK, BLK), 0) == lax.broadcasted_iota(jnp.int32, (BLK, BLK), 1)
    diagonal = [jnp.where(same, pivot[k : k + BLK, k : k + BLK], 0.0) for k in range(0, PW, BLK)]
    diagonal = (diagonal[0] + diagonal[1]) + (diagonal[2] + diagonal[3])
    scale = jnp.sum(jnp.sum(diagonal, axis=0, keepdims=True), axis=1, keepdims=True) / PW
    near = jnp.where(jnp.abs(scale) > 1.0, 2.0**-64, 2.0**64)
    inverse_scale = 1.0 / (scale * near)
    same = lax.broadcasted_iota(jnp.int32, (PW, PW), 0) == lax.broadcasted_iota(jnp.int32, (PW, PW), 1)
    rest_hi, rest_lo = split(jnp.where(same, 1.0, 0.0) - (pivot * near) * inverse_scale)
    row_ids = (gr * NY * NZ + gc) * ROWS + lax.broadcasted_iota(jnp.int32, (ROWS, PW), 0)
    unit = jnp.where(row_ids == lax.broadcasted_iota(jnp.int32, (ROWS, PW), 1), 1.0, 0.0)
    left = jnp.where(row_ids < PW, unit, schur / scale)
    total = left
    for _ in range(POWERS):
        hi, lo = split(total)
        both = jnp.dot(jnp.concatenate([hi, lo]), rest_hi, preferred_element_type=F32)
        total = left + (both[:ROWS] + (both[ROWS:] + jnp.dot(hi, rest_lo, preferred_element_type=F32)))
    out[...] = total

    arrived(ut.at[pl.ds(0, 48), :], sent.at[0])
    arrived(thr.at[:, pl.ds(0, (NY - 1) * KC)], sent.at[1])
    arrived(ut.at[pl.ds(0, 3 * GW), :], sent.at[2])
    arrived(ut.at[pl.ds(0, PW // NC), :], sent.at[3])
    arrived(abuf.at[:, :, pl.ds(0, (NY - 1) * KC)], sent.at[5])
    arrived(codes.at[pl.ds(0, 13)], sent.at[8])
    arrived(steps.at[pl.ds(0, 14)], sent.at[13])
    arrived(spread.at[0, pl.ds(0, NZ - 1), 0], sent.at[10])
    arrived(spread.at[pl.ds(0, NY - 1), :, 0], sent.at[11])
    arrived(spread.at[:, :, 0], sent.at[12])

    @pl.when(pivot_plane)
    def _():
        arrived(mbuf.at[:, pl.ds(0, (NY - 1) * KC)], sent.at[4])
        arrived(mcodes.at[pl.ds(0, NZ - 1)], sent.at[7])
        arrived(msteps.at[pl.ds(0, NZ - 1)], sent.at[14])
        arrived(spread.at[0, pl.ds(0, NZ - 1), 0], sent.at[9])

    @pl.when(jnp.logical_and(gr == 0, gc < 4))
    def _():
        arrived(panel.at[pl.ds(0, 88), :], sent.at[6])

    @pl.when(jnp.logical_and(gr == 0, gc == 4))
    def _():
        arrived(panel.at[pl.ds(0, 96), :], sent.at[6])


def body(window, upper, panel, first):
    vmem, dma = pltpu.VMEM, pltpu.SemaphoreType.DMA
    spec = pl.BlockSpec(memory_space=pltpu.VMEM)

    return pl.pallas_call(
        kernel,
        out_shape=jax.ShapeDtypeStruct((ROWS, PW), F32),
        in_specs=[pl.BlockSpec(memory_space=pltpu.HBM)] * 4,
        out_specs=spec,
        scratch_shapes=[
            pltpu.SMEM((2,), jnp.int32),
            vmem((PW, NY * KC), BF16),
            vmem((8, NY * KC), jnp.int32),
            vmem((ROWS, PW), F32),
            vmem((NZ, ROWS, NY * KC), BF16),
            vmem((BLK, NY * KC), BF16),
            vmem((BLK, PW), F32),
            vmem((2 * NZ - 1, 16, PW), jnp.int16),
            vmem((2 * NZ - 1, 1, PW), F32),
            vmem((2, 8, PW), F32),
            vmem((2, 8, PW), F32),
            vmem((NY, NZ, NC, 8, PW), F32),
            vmem((7, ROWS, PW), F32),
            vmem((32, PARTS[0], PW), jnp.int16),
            vmem((32, 1, PW), F32),
            dma((3,)), dma((15,)),
            dma((NY - 1,)), dma, dma((NX - 1,)), dma, dma((NZ,)), dma, dma, dma, dma, dma,
            dma((NZ - 1,)), dma((NY - 1,)), dma, dma((2, 4, 2)),
        ],
        compiler_params=pltpu.CompilerParams(
            collective_id=0, has_side_effects=True, vmem_limit_bytes=40 * 1024 * 1024
        ),
        name="panel_update",
    )(*[pltpu.with_memory_space_constraint(v, pltpu.HBM) for v in (window, upper.T, panel, first)])


def solution(mesh):
    return jax.shard_map(
        body,
        mesh=mesh,
        in_specs=(P("gr", "gc"), P("gc", "gr"), P(("gr", "gc"), None), P("gc")),
        out_specs=P(("gr", "gc"), None),
        check_vma=False,
    )
```

```python
import jax
import jax.numpy as jnp
from jax import lax
from jax.experimental import pallas as pl
from jax.experimental.pallas import tpu as pltpu
from jax.sharding import PartitionSpec as P

BLK = 128
NX, NC, NY, NZ = 4, 2, 4, 8
PW = 512
ROWS = 104
KC = 256
GW = 64
PARTS = (56, 48)
LEVELS = 32767.0
POWERS = 7
MESH = pl.DeviceIdType.MESH
F32 = jnp.float32
BF16 = jnp.bfloat16


def split(v):
    hi = v.astype(BF16)
    return hi, (v - hi.astype(F32)).astype(BF16)


def coded(v):
    step = jnp.maximum(jnp.max(jnp.abs(v), axis=0, keepdims=True) * (1.0 / LEVELS), 1e-37)
    return jnp.round(v * (1.0 / step)).astype(jnp.int32).astype(jnp.int16), step


def times_transposed(a, bt):
    return lax.dot_general(a, bt, (((1,), (1,)), ((), ())), preferred_element_type=F32)


def kernel(
    window, upper, panel, first_block, out,
    first, ut, thr, pown, abuf, mbuf, msend, mcodes, msteps, ppan, piece, spread,
    sums, codes, steps,
    loc, sent, uy_r, th_r, ux_r, uc_r, a_r, m_r, pan_r, mz_r, mzs_r, xs_r, zs_r, ys_r, cs_r, ring_r,
):
    gr, gc = lax.axis_index("gr"), lax.axis_index("gc")
    x, c = gr // NC, gr % NC
    z, y = gc // NY, gc % NY
    pivot_plane = gr == 0
    panel_source = jnp.logical_and(gr == 0, gc < 5)

    def at_y(d):
        return (gr, z * NY + (y + d) % NY)

    def at_z(d):
        return (gr, ((z + d) % NZ) * NY + y)

    def at_x(d):
        return (((x + d) % NX) * NC + c, gc)

    other_core = (x * NC + 1 - c, gc)

    def at_gr(d):
        return ((gr + d) % (NX * NC), gc)

    def remote(src, dst, s, r, who):
        return pltpu.make_async_remote_copy(
            src_ref=src, dst_ref=dst, send_sem=s, recv_sem=r, device_id=who, device_id_type=MESH
        )

    def arrived(like, sem):
        pltpu.make_async_copy(like, like, sem).wait()

    first_own = pltpu.make_async_copy(first_block, first, loc.at[2])
    first_own.start()

    barrier = pltpu.get_barrier_semaphore()
    for d in range(1, NY):
        pl.semaphore_signal(barrier, inc=1, device_id=at_y(d), device_id_type=MESH)
    for d in range(1, NX * NC):
        pl.semaphore_signal(barrier, inc=1, device_id=at_gr(d), device_id_type=MESH)
    for d in range(1, NZ):
        pl.semaphore_signal(barrier, inc=1, device_id=at_z(d), device_id_type=MESH)
    for s in range(2):
        owner = (16 * y + 2 * z + s) // 13

        @pl.when(jnp.logical_and(pivot_plane, owner != gc))
        def _():
            pl.semaphore_signal(barrier, inc=1, device_id=(0, owner), device_id_type=MESH)

    def group(d):
        return pl.ds((((x + d) % NX) * NC + c) * GW, GW)

    def cols(d):
        return pl.ds(((y + d) % NY) * KC, KC)

    upper_own = pltpu.make_async_copy(upper, ut.at[group(0), cols(0)], loc.at[0])
    upper_own.start()
    lane = lax.broadcasted_iota(jnp.int32, (8, KC), 1)
    first_own.wait()
    thr[:, pl.ds(y * KC, KC)] = jnp.where(lane < BLK, first[0], first[1]) * BLK
    upper_own.wait()

    pl.semaphore_wait(barrier, 17 + jnp.where(panel_source, 11 + gc // 4, 0))

    uy = [remote(ut.at[group(0), cols(0)], ut.at[group(0), cols(0)], sent.at[0], uy_r.at[d - 1], at_y(d)) for d in range(1, NY)]
    th = [
        remote(thr.at[:, cols(0)], thr.at[:, cols(0)], sent.at[1], th_r, at_y(d)) for d in range(1, NY)
    ]
    ux = [
        [
            remote(ut.at[group(0), cols(-j)], ut.at[group(0), cols(-j)],
                   sent.at[2], ux_r.at[d - 1], at_x(d))
            for j in range(NY)
        ]
        for d in range(1, NX)
    ]
    panel_own = pltpu.make_async_copy(panel, pown, loc.at[1])
    for d in (1, 3, 2):
        uy[d - 1].start()
    for d in (1, 3, 2):
        ux[d - 1][0].start()
    for copy in th:
        copy.start()

    mini = [
        remote(window.at[pl.ds(((y + d) % NY) * BLK, BLK), :], mbuf.at[:, pl.ds(y * KC, KC)],
               sent.at[4], m_r, at_y(d))
        for d in range(1, NY)
    ]
    mini_own = pltpu.make_async_copy(window.at[pl.ds(y * BLK, BLK), :], mbuf.at[:, pl.ds(y * KC, KC)], m_r)

    @pl.when(pivot_plane)
    def _():
        for copy in mini:
            copy.start()
        mini_own.start()

    order = (4, 3, 5, 2, 6, 1, 7, 0)

    def rows_of(i, yy):
        return pl.ds(pl.multiple_of((((z + order[i]) % NZ) * NY + yy) * ROWS, 8), ROWS)

    exchange, own_rows = [], []
    for i in range(NZ):
        exchange.append([
            remote(window.at[rows_of(i, (y + d) % NY), :], abuf.at[i, :, pl.ds(y * KC, KC)],
                   sent.at[5], a_r.at[i], at_y(d))
            for d in range(1, NY)
        ])
        own_rows.append(
            pltpu.make_async_copy(window.at[rows_of(i, y), :], abuf.at[i, :, pl.ds(y * KC, KC)], a_r.at[i])
        )
        for copy in exchange[i] if i < NZ - 1 else []:
            copy.start()
        own_rows[i].start()

    panel_own.start()

    def panel_piece(i):
        p = 13 * gc + i
        to = ((p % 16) // 2) * NY + p // 16
        return p, to

    for i in range(13):
        p, to = panel_piece(i)

        @pl.when(jnp.logical_and(jnp.logical_and(panel_source, p < 64), to != gc))
        def _():
            remote(panel.at[pl.ds(8 * i, 8), :], ppan.at[p % 2], sent.at[6], pan_r, (0, to)).start()

        @pl.when(jnp.logical_and(jnp.logical_and(panel_source, p < 64), to == gc))
        def _():
            pltpu.make_async_copy(panel.at[pl.ds(8 * i, 8), :], ppan.at[p % 2], pan_r).start()

    for j in (1, 3, 2):
        uy[j - 1].wait_recv()
        for d in (1, 3, 2):
            ux[d - 1][j].start()
    uc = [remote(ut.at[group(-d), :], ut.at[group(-d), :], sent.at[3], uc_r, other_core) for d in range(NX)]
    uc[0].start()
    for d in (1, 3, 2):
        arrived(ut.at[group(-d), :], ux_r.at[d - 1])
        uc[d].start()
    arrived(thr.at[:, pl.ds(0, (NY - 1) * KC)], th_r)
    arrived(ut.at[pl.ds(0, PW // NC), :], uc_r)

    def product(a, row0):
        ids = row0 + lax.broadcasted_iota(jnp.int32, a.shape, 0)
        kept = jnp.where(ids >= thr[0:1, :], a.astype(F32), 0.0).astype(BF16)
        return times_transposed(kept, ut[...])

    mz = [
        [
            remote(mcodes.at[(z + d) % NZ], mcodes.at[NZ + d - 1], sent.at[7], mz_r, at_z(d)),
            remote(msteps.at[(z + d) % NZ], msteps.at[NZ + d - 1], sent.at[14], mzs_r, at_z(d)),
        ]
        for d in range(1, NZ)
    ]

    @pl.when(pivot_plane)
    def _():
        arrived(mbuf, m_r)
        msend[...] = product(mbuf[...], y * BLK)
        for k in range(NZ):
            mcodes[k], msteps[k] = coded(msend[pl.ds(16 * k, 16), :])
        for d in (4, 3, 5, 2, 6, 1, 7):
            for copy in mz[d - 1]:
                copy.start()

    def chunk(i):
        arrived(abuf.at[i], a_r.at[i])
        return product(abuf[i], gr * (ROWS * NY * NZ) + (((z + order[i]) % NZ) * NY + y) * ROWS)

    parts = (pl.ds(0, PARTS[0]), pl.ds(PARTS[0], PARTS[1]))
    PLUS, MINUS = 0, 1
    hops = (at_z(1), at_z(NZ - 1))

    def message(way, k, h):
        at = 16 * way + 2 * k + h
        rows = pl.ds(0, PARTS[h])
        return [
            remote(codes.at[at, rows, :], codes.at[at + 8, rows, :], sent.at[8], ring_r.at[way, k, h], hops[way]),
            remote(steps.at[at], steps.at[at + 8], sent.at[13], ring_r.at[way, k, h], hops[way]),
        ]

    def send_on(way, k, h, v):
        at = 16 * way + 2 * k + h
        codes[at, pl.ds(0, PARTS[h]), :], steps[at] = coded(v)
        for copy in message(way, k, h):
            copy.start()

    def came(way, k, h):
        at = 16 * way + 2 * k + h + 8
        arrived(steps.at[pl.ds(0, PARTS[h] // 2 + 1)], ring_r.at[way, k, h])
        return codes[at, pl.ds(0, PARTS[h]), :].astype(jnp.int32).astype(F32) * steps[at]

    def forward(k, h):
        send_on(PLUS, k, h, sums[2 * k - 1, parts[h], :] + came(PLUS, k - 1, h))
        send_on(MINUS, k, 1 - h, sums[2 * k, parts[1 - h], :] + came(MINUS, k - 1, 1 - h))

    update = chunk(0)
    send_on(PLUS, 0, 0, update[: PARTS[0]])
    send_on(MINUS, 0, 1, update[PARTS[0] :])
    spread_x = [
        remote(piece.at[(d % NC)], spread.at[y, z, d % NC], sent.at[9], xs_r, (d, gc))
        for d in range(1, NX * NC)
    ]

    spread_z = [
        remote(spread.at[y, z, c], spread.at[y, z, c], sent.at[10], zs_r.at[d - 1], at_z(d)) for d in range(1, NZ)
    ]
    spread_y = [
        [
            remote(spread.at[y, (z + NZ - j) % NZ, c], spread.at[y, (z + NZ - j) % NZ, c],
                   sent.at[11], ys_r.at[d - 1], at_y(d))
            for j in range(NZ)
        ]
        for d in range(1, NY)
    ]

    def spread_own():
        for d in (1, 7, 2, 6, 3, 5, 4):
            spread_z[d - 1].start()
        for d in (1, 3, 2):
            spread_y[d - 1][0].start()
        for copy in exchange[NZ - 1]:
            copy.start()

    @pl.when(pivot_plane)
    def _():
        arrived(mcodes.at[pl.ds(0, NZ - 1)], mz_r)
        arrived(msteps.at[pl.ds(0, NZ - 1)], mzs_r)
        arrived(ppan, pan_r)
        total = msend[pl.ds(z * 16, 16), :]
        for d in range(1, NZ):
            total = total + mcodes[NZ + d - 1].astype(jnp.int32).astype(F32) * msteps[NZ + d - 1]
        for s in range(2):
            piece[s] = ppan[s] - total[8 * s : 8 * s + 8]
        spread[y, z, 0] = piece[0]
        for d in (4, 5, 2, 3, 6, 7, 1):
            spread_x[d - 1].start()
        spread_own()

    sums[1] = chunk(1)
    send_on(PLUS, 1, 1, sums[1, parts[1], :])
    other_planes = jnp.logical_not(pivot_plane)

    def came_along_z(which, where):
        @pl.when(where)
        def _():
            for j in which:
                spread_z[j - 1].wait_recv()
                for d in (1, 3, 2):
                    spread_y[d - 1][j].start()

    sums[2] = chunk(2)
    send_on(MINUS, 1, 0, sums[2, parts[0], :])
    forward(1, 0)
    sums[3] = chunk(3)
    sums[4] = chunk(4)
    came_along_z((1, 7, 2, 6), pivot_plane)
    forward(2, 1)

    @pl.when(jnp.logical_not(pivot_plane))
    def _():
        remote(piece.at[0], spread.at[y, z, c], sent.at[9], xs_r, (0, gc)).wait_recv()
        spread_own()


    came_along_z((3, 5, 4), pivot_plane)
    forward(2, 0)

    came_along_z((1, 7), other_planes)
    sums[5] = chunk(5)
    came_along_z((2, 6), other_planes)
    sums[6] = chunk(6)
    forward(3, 1)
    forward(3, 0)

    came_along_z((3, 5, 4), other_planes)
    spread_c = [
        remote(spread.at[(y + NY - d) % NY, :, c], spread.at[(y + NY - d) % NY, :, c], sent.at[12], cs_r, other_core)
        for d in range(NY)
    ]
    spread_c[0].start()

    def came_along_y(where):
        @pl.when(where)
        def _():
            for d in (1, 3, 2):
                arrived(spread.at[0, :, 0], ys_r.at[d - 1])
                spread_c[d].start()

    came_along_y(gr >= 0)

    sums[0] = chunk(7)
    panel_own.wait()
    for h in (1, 0):
        sums[0, parts[h], :] += came(PLUS, 3, h)
        sums[0, parts[1 - h], :] += came(MINUS, 3, 1 - h)
    schur = pown[...] - sums[0]

    arrived(spread.at[:, :, 0], cs_r)

    pivot = spread[...].reshape(PW, PW)
    same = lax.broadcasted_iota(jnp.int32, (BLK, BLK), 0) == lax.broadcasted_iota(jnp.int32, (BLK, BLK), 1)
    diagonal = [jnp.where(same, pivot[k : k + BLK, k : k + BLK], 0.0) for k in range(0, PW, BLK)]
    diagonal = (diagonal[0] + diagonal[1]) + (diagonal[2] + diagonal[3])
    scale = jnp.sum(jnp.sum(diagonal, axis=0, keepdims=True), axis=1, keepdims=True) / PW
    near = jnp.where(jnp.abs(scale) > 1.0, 2.0**-64, 2.0**64)
    inverse_scale = 1.0 / (scale * near)
    same = lax.broadcasted_iota(jnp.int32, (PW, PW), 0) == lax.broadcasted_iota(jnp.int32, (PW, PW), 1)
    rest_hi, rest_lo = split(jnp.where(same, 1.0, 0.0) - (pivot * near) * inverse_scale)
    row_ids = (gr * NY * NZ + gc) * ROWS + lax.broadcasted_iota(jnp.int32, (ROWS, PW), 0)
    unit = jnp.where(row_ids == lax.broadcasted_iota(jnp.int32, (ROWS, PW), 1), 1.0, 0.0)
    left = jnp.where(row_ids < PW, unit, schur / scale)
    total = left
    for _ in range(POWERS):
        hi, lo = split(total)
        both = jnp.dot(jnp.concatenate([hi, lo]), rest_hi, preferred_element_type=F32)
        total = left + (both[:ROWS] + (both[ROWS:] + jnp.dot(hi, rest_lo, preferred_element_type=F32)))
    out[...] = total

    arrived(ut.at[pl.ds(0, 48), :], sent.at[0])
    arrived(thr.at[:, pl.ds(0, (NY - 1) * KC)], sent.at[1])
    arrived(ut.at[pl.ds(0, 3 * GW), :], sent.at[2])
    arrived(ut.at[pl.ds(0, PW // NC), :], sent.at[3])
    arrived(abuf.at[:, :, pl.ds(0, (NY - 1) * KC)], sent.at[5])
    arrived(codes.at[pl.ds(0, 13)], sent.at[8])
    arrived(steps.at[pl.ds(0, 14)], sent.at[13])
    arrived(spread.at[0, pl.ds(0, NZ - 1), 0], sent.at[10])
    arrived(spread.at[pl.ds(0, NY - 1), :, 0], sent.at[11])
    arrived(spread.at[:, :, 0], sent.at[12])

    @pl.when(pivot_plane)
    def _():
        arrived(mbuf.at[:, pl.ds(0, (NY - 1) * KC)], sent.at[4])
        arrived(mcodes.at[pl.ds(0, NZ - 1)], sent.at[7])
        arrived(msteps.at[pl.ds(0, NZ - 1)], sent.at[14])
        arrived(spread.at[0, pl.ds(0, NZ - 1), 0], sent.at[9])

    @pl.when(jnp.logical_and(gr == 0, gc < 4))
    def _():
        arrived(panel.at[pl.ds(0, 88), :], sent.at[6])

    @pl.when(jnp.logical_and(gr == 0, gc == 4))
    def _():
        arrived(panel.at[pl.ds(0, 96), :], sent.at[6])


def body(window, upper, panel, first):
    vmem, dma = pltpu.VMEM, pltpu.SemaphoreType.DMA
    spec = pl.BlockSpec(memory_space=pltpu.VMEM)

    return pl.pallas_call(
        kernel,
        out_shape=jax.ShapeDtypeStruct((ROWS, PW), F32),
        in_specs=[pl.BlockSpec(memory_space=pltpu.HBM)] * 4,
        out_specs=spec,
        scratch_shapes=[
            pltpu.SMEM((2,), jnp.int32),
            vmem((PW, NY * KC), BF16),
            vmem((8, NY * KC), jnp.int32),
            vmem((ROWS, PW), F32),
            vmem((NZ, ROWS, NY * KC), BF16),
            vmem((BLK, NY * KC), BF16),
            vmem((BLK, PW), F32),
            vmem((2 * NZ - 1, 16, PW), jnp.int16),
            vmem((2 * NZ - 1, 1, PW), F32),
            vmem((2, 8, PW), F32),
            vmem((2, 8, PW), F32),
            vmem((NY, NZ, NC, 8, PW), F32),
            vmem((7, ROWS, PW), F32),
            vmem((32, PARTS[0], PW), jnp.int16),
            vmem((32, 1, PW), F32),
            dma((3,)), dma((15,)),
            dma((NY - 1,)), dma, dma((NX - 1,)), dma, dma((NZ,)), dma, dma, dma, dma, dma,
            dma((NZ - 1,)), dma((NY - 1,)), dma, dma((2, 4, 2)),
        ],
        compiler_params=pltpu.CompilerParams(
            collective_id=0, has_side_effects=True, vmem_limit_bytes=40 * 1024 * 1024
        ),
        name="panel_update",
    )(*[pltpu.with_memory_space_constraint(v, pltpu.HBM) for v in (window, upper.T, panel, first)])


def solution(mesh):
    return jax.shard_map(
        body,
        mesh=mesh,
        in_specs=(P("gr", "gc"), P("gc", "gr"), P(("gr", "gc"), None), P("gc")),
        out_specs=P(("gr", "gc"), None),
        check_vma=False,
    )
```
